256 devices in a mesh: seq: 16 (over x, z_hi, core), chan: 16 (over z_lo, y).
Axes of the slice: x: 4, y: 4, z: 8 (z_hi: 2, z_lo: 4; z = z_hi * 4 + z_lo), core: 2. Of those that a mesh axis runs over, the one named last changes fastest.
Arguments:
- values: bfloat16 [1024, 16384], P('chan', 'seq'), may hold values from -6 to 6
- gate_acts: bfloat16 [1024, 16384], P('chan', 'seq'), may hold values from -6 to 6
- cotangent: bfloat16 [1024, 16384], P('chan', 'seq'), may hold values from -6 to 6
- filter_taps: float32 [1024, 16384], P('chan', 'seq'), may hold values from -160 to 160
- w_value: bfloat16 [1024, 1024], replicated, may hold values from -0.1875 to 0.1875
- w_gate: bfloat16 [1024, 1024], replicated, may hold values from -0.1875 to 0.1875
Outputs:
- input_grad: bfloat16 [16384, 1024], P(('seq', 'chan'))
- filter_grad: float32 [1024, 16384], P('chan', 'seq')
The draws below stay inside these ranges and needn't reach their ends.
All inputs are finite; a program needn't handle non-finite values.
Results may differ from the reference program's by a relative error of at most 0.005.
Values may be sent and summed in bfloat16 or wider, within the bound.
A program may use at most 64 MiB of HBM per device.

```python
import math
import jax
import jax.numpy as jnp
from jax import lax

D = 1024
SEQ = 16384


def draw_filter_taps(key, part):
    keys = jax.random.split(key, 4)
    slow_share = 0.5
    chooser = jax.random.uniform(keys[0], (D, 1), jnp.float32)
    slow_rate = jnp.exp(jax.random.uniform(keys[1], (D, 1), jnp.float32, math.log(0.2 / SEQ), math.log(2.0 / SEQ)))
    fast_rate = jnp.exp(jax.random.uniform(keys[2], (D, 1), jnp.float32, math.log(1.0 / 50.0), math.log(1.0 / 30.0)))
    rate = jnp.where(chooser < slow_share, slow_rate, fast_rate)
    lags = jnp.arange(SEQ, dtype=jnp.float32)[None, :]
    envelope = jnp.exp(-rate * lags)
    energy = jnp.expm1(-2.0 * rate * SEQ) / jnp.expm1(-2.0 * rate)
    amplitude = jnp.sqrt(SEQ / energy)
    noise = jnp.clip(jax.random.normal(keys[3], (D, SEQ), jnp.float32), -4.0, 4.0)
    return jnp.clip(noise * envelope * amplitude, -160.0, 160.0).astype(jnp.float32)


def block_levels(key, shape, shards, low, largest):
    def one(dim, shards_of):
        heights = jax.random.uniform(jax.random.fold_in(jax.random.fold_in(key, 6), dim), (shards_of,), jnp.float32, low / len(shards), largest / len(shards))
        return jnp.repeat(jnp.exp(heights), shape[dim] // shards_of).reshape((-1,) + (1,) * (len(shape) - dim - 1))

    gain = one(*shards[0])
    for cut in shards[1:]:
        gain = gain * one(*cut)
    return gain


def normal_values(stream_key, extent, width, bound, cuts=(), kind=jnp.bfloat16):
    drawn = width * jax.random.normal(stream_key, extent, jnp.float32)
    if cuts:
        drawn = drawn * block_levels(stream_key, extent, cuts, -0.22, 0.18)
    return jnp.clip(drawn, -bound, bound).astype(kind)


def setup_inputs(seed: int = 0) -> dict:
    splits = jax.random.split(jax.random.key(seed), 7)
    return {
        "values": normal_values(splits[0], (D, SEQ), 1.0, 6.0, ((0, 16), (1, 16))),
        "gate_acts": normal_values(splits[1], (D, SEQ), 1.0, 6.0, ((0, 16), (1, 16))),
        "cotangent": normal_values(splits[2], (D, SEQ), 1.0, 6.0, ((0, 16), (1, 16))),
        "filter_taps": draw_filter_taps(jax.random.fold_in(splits[6], 71), 0),
        "w_value": normal_values(splits[4], (D, D), D ** -0.5, 0.1875),
        "w_gate": normal_values(splits[5], (D, D), D ** -0.5, 0.1875),
    }


def block_grads(blocks):
    values, gate_acts, cotangent, filter_taps = blocks
    length = 2 * SEQ
    factor = 1.0 / math.sqrt(SEQ)
    kernel = filter_taps.astype(jnp.float32) * factor
    signal = values.astype(jnp.float32)
    upstream = cotangent.astype(jnp.float32) * gate_acts.astype(jnp.float32)
    kernel_spec = jnp.fft.rfft(kernel, n=length, axis=-1)
    signal_spec = jnp.fft.rfft(signal, n=length, axis=-1)
    upstream_spec = jnp.fft.rfft(upstream, n=length, axis=-1)
    conv_out = jnp.fft.irfft(kernel_spec * signal_spec, n=length, axis=-1)[:, :SEQ]
    value_grad = jnp.fft.irfft(jnp.conj(kernel_spec) * upstream_spec, n=length, axis=-1)[:, :SEQ]
    taps_grad = jnp.fft.irfft(upstream_spec * jnp.conj(signal_spec), n=length, axis=-1)[:, :SEQ] * factor
    gate_grad = cotangent.astype(jnp.float32) * conv_out
    return (value_grad.astype(jnp.bfloat16), gate_grad.astype(jnp.bfloat16), taps_grad.astype(jnp.float32))

def reference(values, gate_acts, cotangent, filter_taps, w_value, w_gate):
    group_size = 64
    blocks_count = D // group_size

    def split_rows(array):
        return array.reshape(blocks_count, group_size, SEQ)
    value_grad, gate_grad, taps_grad = lax.map(block_grads, (split_rows(values), split_rows(gate_acts), split_rows(cotangent), split_rows(filter_taps)))
    value_grad = value_grad.reshape(D, SEQ)
    gate_grad = gate_grad.reshape(D, SEQ)
    input_grad = jnp.dot(value_grad.T, w_value.T, preferred_element_type=jnp.float32)
    input_grad = input_grad + jnp.dot(gate_grad.T, w_gate.T, preferred_element_type=jnp.float32)
    return (input_grad.astype(jnp.bfloat16), taps_grad.reshape(D, SEQ))
```

```python
import numpy as np

import jax
import jax.numpy as jnp
import ml_dtypes
from jax import lax
from jax.sharding import PartitionSpec as P


def dft_matrix(block):
    order = np.concatenate([np.arange(0, block, 2), np.arange(1, block, 2)])
    steps = (2 * order + 1)[None, :] * np.arange(block)[:, None] % (4 * block)
    angle = np.pi * steps / (2 * block)
    return np.concatenate([np.cos(angle), -np.sin(angle)], 1).astype(ml_dtypes.bfloat16)


def local(values, gate_acts, cotangent, filter_taps, w_value, w_gate):
    n_seq = lax.axis_size("seq")
    channels, block = values.shape
    mine = channels // n_seq
    total = block * n_seq
    bf16 = jnp.bfloat16
    f32 = jnp.float32
    table = jnp.asarray(dft_matrix(block))
    upstream = (cotangent.astype(f32) * gate_acts.astype(f32)).astype(bf16)
    packed = jnp.stack([values, upstream, filter_taps.astype(bf16), cotangent])
    packed = packed.reshape(4, n_seq, mine, block).transpose(1, 0, 2, 3)
    got = lax.all_to_all(packed, "seq", split_axis=0, concat_axis=0, tiled=True)
    spectra = lax.dot_general(
        got[:, :3], table, (((3,), (0,)), ((), ())), preferred_element_type=f32
    )
    re = spectra[..., :block]
    im = spectra[..., block:]
    half = block // 2
    sign = jnp.where(jnp.arange(block) < half, 1.0, -1.0)

    def conv(p, q):
        (pr, pi), (qr, qi) = p, q
        out_r = 0.0
        out_i = 0.0
        for c in range(n_seq):
            pad = ((c, 0), (0, 0), (0, 0))
            sr = jnp.pad(qr[: n_seq - c], pad)
            si = jnp.pad(qi[: n_seq - c], pad)
            out_r = out_r + (pr[c] * sr - pi[c] * si)
            out_i = out_i + (pr[c] * si + pi[c] * sr)
        pad = ((1, 0), (0, 0), (0, 0))
        before_r = jnp.pad(out_r[:-1], pad)
        before_i = jnp.pad(out_i[:-1], pad)
        return out_r - sign * before_i, out_i + sign * before_r

    def corr(p, q):
        (pr, pi), (qr, qi) = p, q
        out_r = 0.0
        out_i = 0.0
        for c in range(n_seq):
            pad = ((0, c), (0, 0), (0, 0))
            sr = jnp.pad(qr[c:], pad)
            si = jnp.pad(qi[c:], pad)
            out_r = out_r + (pr[c] * sr + pi[c] * si)
            out_i = out_i + (pr[c] * si - pi[c] * sr)
        pad = ((0, 1), (0, 0), (0, 0))
        after_r = jnp.pad(out_r[1:], pad)
        after_i = jnp.pad(out_i[1:], pad)
        return out_r + sign * after_i, out_i - sign * after_r

    v = (re[:, 0], im[:, 0])
    u = (re[:, 1], im[:, 1])
    h = (re[:, 2], im[:, 2])
    triples = [conv(h, v), corr(h, u), corr(v, u)]
    products = jnp.stack([jnp.concatenate(t, -1).astype(bf16) for t in triples], 1)
    signals = lax.dot_general(
        products, table, (((3,), (1,)), ((), ())), preferred_element_type=f32
    )
    signals = signals * (1.0 / (block * total**0.5))
    gate_grad = got[:, 3].astype(f32) * signals[:, 0]
    back = jnp.stack([signals[:, 1], gate_grad, signals[:, 2]], 1).astype(bf16)
    back = lax.all_to_all(back, "seq", split_axis=0, concat_axis=0, tiled=True)
    back = back.transpose(1, 0, 2, 3).reshape(3, channels, block)
    grads = lax.all_to_all(back[:2], "chan", split_axis=2, concat_axis=1, tiled=True)
    contract = (((0,), (1,)), ((), ()))
    input_grad = lax.dot_general(grads[0], w_value, contract, preferred_element_type=f32)
    input_grad = input_grad + lax.dot_general(
        grads[1], w_gate, contract, preferred_element_type=f32
    )
    return (input_grad.astype(bf16), back[2].astype(f32))


def solution(mesh):
    return jax.shard_map(
        local,
        mesh=mesh,
        in_specs=(P("chan", "seq"), P("chan", "seq"), P("chan", "seq"), P("chan", "seq"), P(), P()),
        out_specs=(P(("seq", "chan"), None), P("chan", "seq")),
        check_vma=False,
    )
```

```python
import functools

import numpy as np

import jax
import jax.numpy as jnp
import ml_dtypes
from jax import lax
from jax.experimental import pallas as pl
from jax.experimental.pallas import tpu as pltpu
from jax.sharding import PartitionSpec as P

MESH = pl.DeviceIdType.MESH
LANES = 128
MINE = 4


def dft_tables(block):
    chunks = block // LANES
    order = np.concatenate([np.arange(0, block, 2), np.arange(1, block, 2)])
    steps = (2 * order + 1)[None, :] * np.arange(block)[:, None] % (4 * block)
    angle = np.pi * steps / (2 * block)
    table = np.stack([np.cos(angle), -np.sin(angle)]).reshape(2, block, chunks, LANES)
    table = table.transpose(2, 1, 0, 3).reshape(chunks, block, 2 * LANES)
    high = table.astype(ml_dtypes.bfloat16)
    low = (table - high.astype(np.float64)).astype(ml_dtypes.bfloat16)
    return high, low


def kernel(
    n_seq,
    n_chan,
    values,
    gates,
    cotangent,
    taps,
    high_hbm,
    low_hbm,
    wv_hbm,
    wg_hbm,
    input_grad,
    filter_grad,
    high,
    low,
    wv,
    wg,
    flat,
    send_hv,
    send_uc,
    got_hv,
    got_uc,
    rows,
    spec,
    swapped,
    prod,
    packed,
    signal,
    send_g,
    send_f,
    got_g,
    got_f,
    tiles,
    stacked,
    load_sem,
    own_sem,
    hv_send,
    hv_recv,
    uc_send,
    uc_recv,
    g_send,
    g_recv,
    f_send,
    f_recv,
    t_send,
    t_recv,
):
    f32 = jnp.float32
    bf16 = jnp.bfloat16
    me = lax.axis_index("seq")
    my_chan = lax.axis_index("chan")
    block = values.shape[1]
    chunks = block // LANES
    share = block // n_chan

    barrier = pltpu.get_barrier_semaphore()

    def greet_seq(k, carry):
        pl.semaphore_signal(
            barrier, inc=1, device_id={"seq": me ^ k}, device_id_type=MESH
        )
        return carry

    def greet_chan(k, carry):
        pl.semaphore_signal(
            barrier, inc=1, device_id={"chan": my_chan ^ k}, device_id_type=MESH
        )
        return carry

    lax.fori_loop(1, n_seq, greet_seq, 0)
    lax.fori_loop(1, n_chan, greet_chan, 0)

    loads = [
        pltpu.make_async_copy(src, dst, load_sem.at[i])
        for i, (src, dst) in enumerate(
            ((high_hbm, high), (low_hbm, low), (wv_hbm, wv), (wg_hbm, wg))
        )
    ]
    for load in loads:
        load.start()

    flat[0] = taps[...]
    flat[1] = values[...].astype(f32)
    cot = cotangent[...].astype(f32)
    flat[2] = cot * gates[...].astype(f32)
    flat[3] = cot

    def pack(t, carry):
        at = pl.ds(pl.multiple_of(t * 8, 8), 8)
        h, v, u, c = (flat[i, at, :] for i in range(4))
        for side in range(2):
            part = slice(side * MINE, side * MINE + MINE)
            hv = jnp.concatenate([h[part], v[part]], 0)
            uc = jnp.concatenate([u[part], c[part]], 0)
            send_hv[2 * t + side] = hv.astype(bf16)
            send_uc[2 * t + side] = uc.astype(bf16)
        return carry

    lax.fori_loop(0, n_seq // 2, pack, 0)
    pl.semaphore_wait(barrier, n_seq + n_chan - 2)

    def to_seq(src, dst, send_sem, recv_sem, peer, slot):
        return pltpu.make_async_remote_copy(
            src_ref=src.at[peer],
            dst_ref=dst.at[slot],
            send_sem=send_sem.at[peer],
            recv_sem=recv_sem.at[slot],
            device_id={"seq": peer},
            device_id_type=MESH,
        )

    def send_all(src, dst, send_sem, recv_sem):
        def step(k, carry):
            to_seq(src, dst, send_sem, recv_sem, me ^ k, me).start()
            return carry

        lax.fori_loop(1, n_seq, step, 0)

    def wait_all(src, dst, send_sem, recv_sem):
        def step(k, carry):
            copy = to_seq(src, dst, send_sem, recv_sem, me ^ k, me ^ k)
            copy.wait_send()
            copy.wait_recv()
            return carry

        lax.fori_loop(1, n_seq, step, 0)

    own_hv = pltpu.make_async_copy(send_hv.at[me], got_hv.at[me], own_sem.at[0])
    own_uc = pltpu.make_async_copy(send_uc.at[me], got_uc.at[me], own_sem.at[1])
    send_all(send_hv, got_hv, hv_send, hv_recv)
    send_all(send_uc, got_uc, uc_send, uc_recv)
    own_hv.start()
    own_uc.start()
    loads[0].wait()
    loads[1].wait()
    own_hv.wait()
    own_uc.wait()
    wait_all(send_hv, got_hv, hv_send, hv_recv)
    wait_all(send_uc, got_uc, uc_send, uc_recv)

    def build(a, carry):
        u = got_uc[a].astype(f32)[:MINE]
        tile = jnp.concatenate([got_hv[a].astype(f32), u, u], 0)
        rows[pl.ds(pl.multiple_of(a * 16, 16), 16), :] = tile.astype(bf16)
        return carry

    lax.fori_loop(0, n_seq, build, 0)

    re = slice(0, LANES)
    im = slice(LANES, 2 * LANES)
    group = 4

    def frequency(j, carry):
        lhs = rows[...]
        spec[...] = jnp.dot(lhs, high[j], preferred_element_type=f32) + jnp.dot(
            lhs, low[j], preferred_element_type=f32
        )
        sign = jnp.where(j < chunks // 2, 1.0, -1.0).astype(f32)

        def first(a):
            at = slice(a * 16, a * 16 + 8)
            return spec[at, re], spec[at, im]

        def second(a):
            at = slice(a * 16 + 8, a * 16 + 16)
            return spec[at, re], spec[at, im]

        for a in range(n_seq):
            at = slice(a * 8, a * 8 + 8)
            pr, pi = first(a)
            swapped[at, re] = pltpu.roll(pr, 4, axis=0)
            swapped[at, im] = pltpu.roll(pi, 4, axis=0)

        def turned(a):
            at = slice(a * 8, a * 8 + 8)
            return swapped[at, re], swapped[at, im]

        before = None
        for base in range(0, n_seq, group):
            acc = [None] * group
            for x in range((base + group - 1) // 2 + 1):
                pr, pi = first(x)
                for i in range(group):
                    y = base + i - x
                    if y < x:
                        continue
                    qr, qi = turned(y)
                    if y == x:
                        ar, ai = pr * 0.5, pi * 0.5
                    else:
                        ar, ai = pr, pi
                    tr = ar * qr - ai * qi
                    ti = ar * qi + ai * qr
                    acc[i] = (tr, ti) if acc[i] is None else (acc[i][0] + tr, acc[i][1] + ti)
            for i in range(group):
                zr, zi = acc[i]
                at = slice((base + i) * 16, (base + i) * 16 + 8)
                if before is None:
                    prod[at, re] = zr
                    prod[at, im] = zi
                else:
                    prod[at, re] = zr - sign * before[1]
                    prod[at, im] = zi + sign * before[0]
                before = (zr, zi)

        after = None
        for base in reversed(range(0, n_seq, group)):
            acc = [None] * group
            for c in range(n_seq - base):
                pr, pi = first(c)
                for i in range(group):
                    if base + i + c >= n_seq:
                        continue
                    qr, qi = second(base + i + c)
                    tr = pr * qr + pi * qi
                    ti = pr * qi - pi * qr
                    acc[i] = (tr, ti) if acc[i] is None else (acc[i][0] + tr, acc[i][1] + ti)
            for i in reversed(range(group)):
                zr, zi = acc[i]
                at = slice((base + i) * 16 + 8, (base + i) * 16 + 16)
                if after is None:
                    prod[at, re] = zr
                    prod[at, im] = zi
                else:
                    prod[at, re] = zr + sign * after[1]
                    prod[at, im] = zi - sign * after[0]
                after = (zr, zi)
        packed[j] = prod[...].astype(bf16)
        return carry

    lax.fori_loop(0, chunks, frequency, 0)

    wide = 256
    turn = (((1,), (1,)), ((), ()))

    def inverse(t, carry):
        at = pl.ds(pl.multiple_of(t * wide, wide), wide)
        total = None
        for j in range(chunks):
            lhs = packed[j]
            part = lax.dot_general(lhs, high[j, at, :], turn, preferred_element_type=f32)
            part = part + lax.dot_general(
                lhs, low[j, at, :], turn, preferred_element_type=f32
            )
            total = part if total is None else total + part
        signal[:, at] = total * (1.0 / (block * 128.0))
        return carry

    lax.fori_loop(0, block // wide, inverse, 0)

    low_lanes = lax.broadcasted_iota(jnp.int32, (MINE, LANES), 1) < share

    def finish(a):
        both = signal[pl.ds(pl.multiple_of(a * 16, 8), 8), :]
        grads = signal[pl.ds(pl.multiple_of(a * 16 + 8, 8), 8), :]
        conv = both[:MINE] + both[MINE:]
        cots = got_uc[a].astype(f32)[MINE:]
        gate_grad = conv * cots
        value_grad = grads[:MINE]
        send_f[a] = grads[MINE:].astype(bf16)
        for p in range(block // LANES):
            at = slice(p * LANES, (p + 1) * LANES)
            x = value_grad[:, at]
            y = gate_grad[:, at]
            even = jnp.where(low_lanes, x, pltpu.roll(y, share, axis=1))
            odd = jnp.where(low_lanes, pltpu.roll(x, share, axis=1), y)
            send_g[a, :, 2 * p * LANES : (2 * p + 1) * LANES] = even.astype(bf16)
            send_g[a, :, (2 * p + 1) * LANES : (2 * p + 2) * LANES] = odd.astype(bf16)

    own_g = pltpu.make_async_copy(send_g.at[me], got_g.at[me], own_sem.at[2])
    own_f = pltpu.make_async_copy(send_f.at[me], got_f.at[me], own_sem.at[3])

    def finish_and_send(k, carry):
        finish(me ^ k)
        to_seq(send_g, got_g, g_send, g_recv, me ^ k, me).start()
        return carry

    lax.fori_loop(1, n_seq, finish_and_send, 0)
    finish(me)
    own_g.start()
    own_f.start()
    send_all(send_f, got_f, f_send, f_recv)
    own_g.wait()
    wait_all(send_g, got_g, g_send, g_recv)

    def to_chan(peer, slot):
        at = pl.ds(pl.multiple_of(peer * LANES, LANES), LANES)
        return pltpu.make_async_remote_copy(
            src_ref=got_g.at[:, :, at],
            dst_ref=tiles.at[slot],
            send_sem=t_send.at[peer],
            recv_sem=t_recv.at[slot],
            device_id={"chan": peer},
            device_id_type=MESH,
        )

    def send_tiles(k, carry):
        to_chan(my_chan ^ k, my_chan).start()
        return carry

    lax.fori_loop(1, n_chan, send_tiles, 0)
    mine_at = pl.ds(pl.multiple_of(my_chan * LANES, LANES), LANES)
    own_t = pltpu.make_async_copy(got_g.at[:, :, mine_at], tiles.at[my_chan], own_sem.at[4])
    own_t.start()

    own_f.wait()
    wait_all(send_f, got_f, f_send, f_recv)

    def unpack(t, carry):
        at = pl.ds(pl.multiple_of(t * 8, 8), 8)
        pair = [got_f[2 * t + side].astype(f32) for side in range(2)]
        filter_grad[at, :] = jnp.concatenate(pair, 0)
        return carry

    lax.fori_loop(0, n_seq // 2, unpack, 0)
    loads[2].wait()
    loads[3].wait()
    own_t.wait()

    def wait_tiles(k, carry):
        copy = to_chan(my_chan ^ k, my_chan ^ k)
        copy.wait_send()
        copy.wait_recv()
        return carry

    lax.fori_loop(1, n_chan, wait_tiles, 0)

    def restack(c, carry):
        for q in range(n_seq // 4):
            tile = jnp.concatenate(
                [tiles[c, 4 * q + i].astype(f32) for i in range(4)], 0
            )
            at = pl.ds(pl.multiple_of(c * 64 + q * 16, 16), 16)
            stacked[at, :] = tile.astype(bf16)
        return carry

    lax.fori_loop(0, n_chan, restack, 0)
    tokens = stacked[...].T
    out = lax.dot_general(tokens[:share], wv[...], turn, preferred_element_type=f32)
    out = out + lax.dot_general(tokens[share:], wg[...], turn, preferred_element_type=f32)
    input_grad[...] = out.astype(bf16)


def solution(mesh):
    n_seq = mesh.shape["seq"]
    n_chan = mesh.shape["chan"]
    bf16 = jnp.bfloat16
    f32 = jnp.float32

    def local(values, gate_acts, cotangent, filter_taps, w_value, w_gate):
        channels, block = values.shape
        chunks = block // LANES
        model = w_value.shape[0]
        high, low = dft_tables(block)
        vmem = pl.BlockSpec(memory_space=pltpu.VMEM)
        anywhere = pl.BlockSpec(memory_space=pl.ANY)
        sems = pltpu.SemaphoreType.DMA
        return pl.pallas_call(
            functools.partial(kernel, n_seq, n_chan),
            out_shape=(
                jax.ShapeDtypeStruct((block // n_chan, model), bf16),
                jax.ShapeDtypeStruct((channels, block), f32),
            ),
            in_specs=[vmem] * 4 + [anywhere] * 4,
            out_specs=(vmem, vmem),
            scratch_shapes=[
                pltpu.VMEM((chunks, block, 2 * LANES), bf16),
                pltpu.VMEM((chunks, block, 2 * LANES), bf16),
                pltpu.VMEM((model, model), bf16),
                pltpu.VMEM((model, model), bf16),
                pltpu.VMEM((4, channels, block), f32),
                pltpu.VMEM((n_seq, 8, block), bf16),
                pltpu.VMEM((n_seq, 8, block), bf16),
                pltpu.VMEM((n_seq, 8, block), bf16),
                pltpu.VMEM((n_seq, 8, block), bf16),
                pltpu.VMEM((n_seq * 16, block), bf16),
                pltpu.VMEM((n_seq * 16, 2 * LANES), f32),
                pltpu.VMEM((n_seq * 8, 2 * LANES), f32),
                pltpu.VMEM((n_seq * 16, 2 * LANES), f32),
                pltpu.VMEM((chunks, n_seq * 16, 2 * LANES), bf16),
                pltpu.VMEM((n_seq * 16, block), f32),
                pltpu.VMEM((n_seq, MINE, 2 * block), bf16),
                pltpu.VMEM((n_seq, MINE, block), bf16),
                pltpu.VMEM((n_seq, MINE, 2 * block), bf16),
                pltpu.VMEM((n_seq, MINE, block), bf16),
                pltpu.VMEM((n_chan, n_seq, MINE, LANES), bf16),
                pltpu.VMEM((model, LANES), bf16),
                sems((4,)),
                sems((5,)),
            ]
            + [sems((n_seq,))] * 8
            + [sems((n_chan,))] * 2,
            compiler_params=pltpu.CompilerParams(
                collective_id=0, has_side_effects=True, vmem_limit_bytes=48 * 1024 * 1024
            ),
        )(
            values,
            gate_acts,
            cotangent,
            filter_taps,
            jnp.asarray(high),
            jnp.asarray(low),
            w_value,
            w_gate,
        )

    return jax.shard_map(
        local,
        mesh=mesh,
        in_specs=(P("chan", "seq"), P("chan", "seq"), P("chan", "seq"), P("chan", "seq"), P(), P()),
        out_specs=(P(("seq", "chan"), None), P("chan", "seq")),
        check_vma=False,
    )
```

```python
import functools

import numpy as np

import jax
import jax.numpy as jnp
import ml_dtypes
from jax import lax
from jax.experimental import pallas as pl
from jax.experimental.pallas import tpu as pltpu
from jax.sharding import PartitionSpec as P

MESH = pl.DeviceIdType.MESH
LANES = 128
MINE = 4


def dft_tables(block):
    chunks = block // LANES
    order = np.concatenate([np.arange(0, block, 2), np.arange(1, block, 2)])
    steps = (2 * order + 1)[None, :] * np.arange(block)[:, None] % (4 * block)
    angle = np.pi * steps / (2 * block)
    table = np.stack([np.cos(angle), -np.sin(angle)]).reshape(2, block, chunks, LANES)
    table = table.transpose(2, 1, 0, 3).reshape(chunks, block, 2 * LANES)
    high = table.astype(ml_dtypes.bfloat16)
    low = (table - high.astype(np.float64)).astype(ml_dtypes.bfloat16)
    return high, low


def kernel(
    n_seq,
    n_chan,
    values_hbm,
    gates_hbm,
    cotangent_hbm,
    taps_hbm,
    high_hbm,
    low_hbm,
    wv_hbm,
    wg_hbm,
    input_grad,
    filter_grad,
    values,
    gates,
    cotangent,
    taps,
    high,
    low,
    wv,
    wg,
    flat,
    send_hv,
    send_u,
    send_c,
    got_hv,
    got_u,
    got_c,
    rows,
    spec,
    swapped,
    doubled,
    prod,
    packed,
    signal,
    send_t,
    send_f,
    got_f,
    tiles,
    stacked,
    load_sem,
    own_sem,
    hv_send,
    hv_recv,
    u_send,
    u_recv,
    c_send,
    c_recv,
    f_send,
    f_recv,
    t_send,
    t_recv,
    met,
):
    f32 = jnp.float32
    bf16 = jnp.bfloat16
    me = lax.axis_index("seq")
    my_chan = lax.axis_index("chan")
    block = values.shape[1]
    chunks = block // LANES
    share = block // n_chan
    pairs = n_seq // 2

    loads = [
        pltpu.make_async_copy(src, dst, load_sem.at[i])
        for i, (src, dst) in enumerate(
            (
                (taps_hbm, taps),
                (values_hbm, values),
                (gates_hbm, gates),
                (cotangent_hbm, cotangent),
                (high_hbm, high),
                (low_hbm, low),
                (wv_hbm, wv),
                (wg_hbm, wg),
            )
        )
    ]
    for load in loads:
        load.start()

    barrier = pltpu.get_barrier_semaphore()

    def greet_seq(k, carry):
        pl.semaphore_signal(
            barrier, inc=1, device_id={"seq": me ^ k}, device_id_type=MESH
        )
        return carry

    def greet_chan(k, carry):
        pl.semaphore_signal(
            barrier, inc=1, device_id={"chan": my_chan ^ k}, device_id_type=MESH
        )
        return carry

    lax.fori_loop(1, n_seq, greet_seq, 0)
    lax.fori_loop(1, n_chan, greet_chan, 0)

    for load in loads[:4]:
        load.wait()
    flat[0] = taps[...]
    flat[1] = values[...].astype(f32)
    cot = cotangent[...].astype(f32)
    flat[2] = cot * gates[...].astype(f32)
    flat[3] = cot

    def pack(t, carry):
        at = pl.ds(pl.multiple_of(t * 8, 8), 8)
        h, v, u, c = (flat[i, at, :] for i in range(4))
        for side in range(2):
            part = slice(side * MINE, side * MINE + MINE)
            hv = jnp.concatenate([h[part], v[part]], 0)
            send_hv[2 * t + side] = hv.astype(bf16)
            send_u[2 * t + side] = u[part].astype(bf16)
            send_c[2 * t + side] = c[part].astype(bf16)
        return carry

    lax.fori_loop(0, pairs, pack, 0)
    pl.semaphore_wait(barrier, n_seq + n_chan - 2)

    def pair_of(i):
        return (me // 2) ^ (2 * (i % (pairs // 2)) + 1 - i // (pairs // 2))

    def to_seq(src, dst, send_sem, recv_sem, peer, slot):
        return pltpu.make_async_remote_copy(
            src_ref=src.at[peer],
            dst_ref=dst.at[slot],
            send_sem=send_sem.at[peer],
            recv_sem=recv_sem.at[slot],
            device_id={"seq": peer},
            device_id_type=MESH,
        )

    def send_all(src, dst, send_sem, recv_sem):
        def step(i, carry):
            for side in range(2):
                peer = 2 * pair_of(i) + side

                @pl.when(peer != me)
                def _():
                    to_seq(src, dst, send_sem, recv_sem, peer, me).start()

            return carry

        lax.fori_loop(0, pairs, step, 0)

    def wait_all(src, dst, send_sem, recv_sem):
        def step(k, carry):
            copy = to_seq(src, dst, send_sem, recv_sem, me ^ k, me ^ k)
            copy.wait_send()
            copy.wait_recv()
            return carry

        lax.fori_loop(1, n_seq, step, 0)

    send_all(send_hv, got_hv, hv_send, hv_recv)
    send_all(send_u, got_u, u_send, u_recv)
    send_all(send_c, got_c, c_send, c_recv)
    own = [
        pltpu.make_async_copy(src.at[me], dst.at[me], own_sem.at[i])
        for i, (src, dst) in enumerate(
            ((send_hv, got_hv), (send_u, got_u), (send_c, got_c))
        )
    ]
    for copy in own:
        copy.start()

    def met_chan(k, carry):
        pl.semaphore_signal(met, inc=1, device_id={"chan": my_chan ^ k}, device_id_type=MESH)
        return carry

    lax.fori_loop(1, n_chan, met_chan, 0)
    loads[4].wait()
    loads[5].wait()
    own[0].wait()
    wait_all(send_hv, got_hv, hv_send, hv_recv)

    def build_hv(t, carry):
        tile = jnp.concatenate([got_hv[2 * t + i].astype(f32) for i in range(2)], 0)
        rows[pl.ds(pl.multiple_of(t * 16, 16), 16), :] = tile.astype(bf16)
        return carry

    lax.fori_loop(0, pairs, build_hv, 0)
    own[1].wait()
    wait_all(send_u, got_u, u_send, u_recv)

    def build_u(t, carry):
        tile = jnp.concatenate([got_u[4 * t + i].astype(f32) for i in range(4)], 0)
        at = pl.ds(pl.multiple_of(n_seq * 8 + t * 16, 16), 16)
        rows[at, :] = tile.astype(bf16)
        return carry

    lax.fori_loop(0, n_seq // 4, build_u, 0)

    re = slice(0, LANES)
    im = slice(LANES, 2 * LANES)
    group = 4
    upper = lax.broadcasted_iota(jnp.int32, (8, LANES), 0) < MINE
    tail = n_seq * 8

    def frequency(j, carry):
        lhs = rows[...]
        spec[...] = jnp.dot(lhs, high[j], preferred_element_type=f32) + jnp.dot(
            lhs, low[j], preferred_element_type=f32
        )
        sign = jnp.where(j < chunks // 2, 1.0, -1.0).astype(f32)

        def first(a):
            at = slice(a * 8, a * 8 + 8)
            return spec[at, re], spec[at, im]

        def second(a):
            at = slice(a * 8, a * 8 + 8)
            return doubled[at, re], doubled[at, im]

        def turned(a):
            at = slice(a * 8, a * 8 + 8)
            return swapped[at, re], swapped[at, im]

        for a in range(n_seq):
            at = slice(a * 8, a * 8 + 8)
            for half in (re, im):
                swapped[at, half] = pltpu.roll(spec[at, half], MINE, axis=0)
        for a in range(0, n_seq, 2):
            for half in (re, im):
                tile = spec[tail + a * 4 : tail + a * 4 + 8, half]
                other = pltpu.roll(tile, MINE, axis=0)
                doubled[a * 8 : a * 8 + 8, half] = jnp.where(upper, tile, other)
                doubled[a * 8 + 8 : a * 8 + 16, half] = jnp.where(upper, other, tile)

        before = None
        for base in range(0, n_seq, group):
            acc = [None] * group
            for x in range((base + group - 1) // 2 + 1):
                pr, pi = first(x)
                for i in range(group):
                    y = base + i - x
                    if y < x:
                        continue
                    qr, qi = turned(y)
                    if y == x:
                        ar, ai = pr * 0.5, pi * 0.5
                    else:
                        ar, ai = pr, pi
                    tr = ar * qr - ai * qi
                    ti = ar * qi + ai * qr
                    acc[i] = (tr, ti) if acc[i] is None else (acc[i][0] + tr, acc[i][1] + ti)
            done = []
            for i in range(group):
                zr, zi = (z + pltpu.roll(z, MINE, axis=0) for z in acc[i])
                if before is None:
                    done.append((zr, zi))
                else:
                    done.append((zr - sign * before[1], zi + sign * before[0]))
                before = (zr, zi)
            for i in range(0, group, 2):
                at = slice(tail + (base + i) * 4, tail + (base + i) * 4 + 8)
                for half, part in ((re, 0), (im, 1)):
                    prod[at, half] = jnp.where(upper, done[i][part], done[i + 1][part])

        after = None
        for base in reversed(range(0, n_seq, group)):
            acc = [None] * group
            for c in range(n_seq - base):
                pr, pi = first(c)
                for i in range(group):
                    if base + i + c >= n_seq:
                        continue
                    qr, qi = second(base + i + c)
                    tr = pr * qr + pi * qi
                    ti = pr * qi - pi * qr
                    acc[i] = (tr, ti) if acc[i] is None else (acc[i][0] + tr, acc[i][1] + ti)
            for i in reversed(range(group)):
                zr, zi = acc[i]
                at = slice((base + i) * 8, (base + i) * 8 + 8)
                if after is None:
                    prod[at, re] = zr
                    prod[at, im] = zi
                else:
                    prod[at, re] = zr + sign * after[1]
                    prod[at, im] = zi - sign * after[0]
                after = (zr, zi)
        packed[j] = prod[...].astype(bf16)
        return carry

    lax.fori_loop(0, chunks, frequency, 0)

    own[2].wait()
    wait_all(send_c, got_c, c_send, c_recv)
    pl.semaphore_wait(met, n_chan - 1)

    wide = 256
    turn = (((1,), (1,)), ((), ()))
    low_lanes = lax.broadcasted_iota(jnp.int32, (MINE, LANES), 1) < share
    per_step = wide // share

    def to_owner(a, c):
        return pltpu.make_async_remote_copy(
            src_ref=send_t.at[a, c],
            dst_ref=tiles.at[my_chan, me],
            send_sem=t_send,
            recv_sem=t_recv,
            device_id={"seq": a, "chan": c},
            device_id_type=MESH,
        )

    def inverse(t, carry):
        at = pl.ds(pl.multiple_of(t * wide, wide), wide)
        total = None
        for j in range(chunks):
            lhs = packed[j]
            part = lax.dot_general(lhs, high[j, at, :], turn, preferred_element_type=f32)
            part = part + lax.dot_general(
                lhs, low[j, at, :], turn, preferred_element_type=f32
            )
            total = part if total is None else total + part
        signal[...] = total * (1.0 / (block * 128.0))

        def finish(i, carry):
            pair = pair_of(i)
            convs = signal[pl.ds(pl.multiple_of(tail + pair * 8, 8), 8), :]
            for side in range(2):
                a = 2 * pair + side
                grads = signal[pl.ds(pl.multiple_of(a * 8, 8), 8), :]
                conv = convs[side * MINE : side * MINE + MINE]
                gate_grad = conv * got_c[a, :, at].astype(f32)
                value_grad = grads[:MINE]
                send_f[a, t] = grads[MINE:].astype(bf16)
                for p in range(wide // LANES):
                    lane = slice(p * LANES, (p + 1) * LANES)
                    x = value_grad[:, lane]
                    y = gate_grad[:, lane]
                    even = jnp.where(low_lanes, x, pltpu.roll(y, share, axis=1))
                    odd = jnp.where(low_lanes, pltpu.roll(x, share, axis=1), y)
                    c = t * per_step + 2 * p
                    send_t[a, c] = even.astype(bf16)
                    send_t[a, c + 1] = odd.astype(bf16)
                for q in range(per_step):
                    c = t * per_step + q

                    @pl.when((a != me) | (c != my_chan))
                    def _():
                        to_owner(a, c).start()

            return carry

        lax.fori_loop(0, pairs, finish, 0)
        return carry

    lax.fori_loop(0, block // wide, inverse, 0)

    own_t = pltpu.make_async_copy(send_t.at[me, my_chan], tiles.at[my_chan, me], t_recv)
    own_f = pltpu.make_async_copy(send_f.at[me], got_f.at[me], own_sem.at[3])
    own_t.start()
    own_f.start()
    send_all(send_f, got_f, f_send, f_recv)
    loads[6].wait()
    loads[7].wait()

    pltpu.make_async_copy(tiles, tiles, t_recv).wait()

    def restack(c, carry):
        for q in range(n_seq // 4):
            tile = jnp.concatenate(
                [tiles[c, 4 * q + i].astype(f32) for i in range(4)], 0
            )
            at = pl.ds(pl.multiple_of(c * 64 + q * 16, 16), 16)
            stacked[at, :] = tile.astype(bf16)
        return carry

    lax.fori_loop(0, n_chan, restack, 0)
    tokens = stacked[...].T
    out = lax.dot_general(tokens[:share], wv[...], turn, preferred_element_type=f32)
    out = out + lax.dot_general(tokens[share:], wg[...], turn, preferred_element_type=f32)
    input_grad[...] = out.astype(bf16)

    own_f.wait()
    wait_all(send_f, got_f, f_send, f_recv)

    def unpack(i, carry):
        at = pl.ds(pl.multiple_of(i * 8, 8), 8)
        for t in range(block // wide):
            pair = [got_f[2 * i + side, t].astype(f32) for side in range(2)]
            filter_grad[at, t * wide : (t + 1) * wide] = jnp.concatenate(pair, 0)
        return carry

    lax.fori_loop(0, pairs, unpack, 0)

    def drain(k, carry):
        pltpu.make_async_copy(send_t.at[k], send_t.at[k], t_send).wait()
        return carry

    lax.fori_loop(1, n_seq, drain, 0)
    rest = send_t.at[0, pl.ds(0, n_chan - 1)]
    pltpu.make_async_copy(rest, rest, t_send).wait()


def solution(mesh):
    n_seq = mesh.shape["seq"]
    n_chan = mesh.shape["chan"]
    bf16 = jnp.bfloat16
    f32 = jnp.float32

    def local(values, gate_acts, cotangent, filter_taps, w_value, w_gate):
        channels, block = values.shape
        chunks = block // LANES
        model = w_value.shape[0]
        high, low = dft_tables(block)
        vmem = pl.BlockSpec(memory_space=pltpu.VMEM)
        hbm = pl.BlockSpec(memory_space=pltpu.MemorySpace.HBM)
        sems = pltpu.SemaphoreType.DMA
        return pl.pallas_call(
            functools.partial(kernel, n_seq, n_chan),
            out_shape=(
                jax.ShapeDtypeStruct((block // n_chan, model), bf16),
                jax.ShapeDtypeStruct((channels, block), f32),
            ),
            in_specs=[hbm] * 8,
            out_specs=(vmem, vmem),
            scratch_shapes=[
                pltpu.VMEM((channels, block), bf16),
                pltpu.VMEM((channels, block), bf16),
                pltpu.VMEM((channels, block), bf16),
                pltpu.VMEM((channels, block), f32),
                pltpu.VMEM((chunks, block, 2 * LANES), bf16),
                pltpu.VMEM((chunks, block, 2 * LANES), bf16),
                pltpu.VMEM((model, model), bf16),
                pltpu.VMEM((model, model), bf16),
                pltpu.VMEM((4, channels, block), f32),
                pltpu.VMEM((n_seq, 2 * MINE, block), bf16),
                pltpu.VMEM((n_seq, MINE, block), bf16),
                pltpu.VMEM((n_seq, MINE, block), bf16),
                pltpu.VMEM((n_seq, 2 * MINE, block), bf16),
                pltpu.VMEM((n_seq, MINE, block), bf16),
                pltpu.VMEM((n_seq, MINE, block), bf16),
                pltpu.VMEM((n_seq * 12, block), bf16),
                pltpu.VMEM((n_seq * 12, 2 * LANES), f32),
                pltpu.VMEM((n_seq * 8, 2 * LANES), f32),
                pltpu.VMEM((n_seq * 8, 2 * LANES), f32),
                pltpu.VMEM((n_seq * 12, 2 * LANES), f32),
                pltpu.VMEM((chunks, n_seq * 12, 2 * LANES), bf16),
                pltpu.VMEM((n_seq * 12, 256), f32),
                pltpu.VMEM((n_seq, n_chan, MINE, LANES), bf16),
                pltpu.VMEM((n_seq, block // 256, MINE, 256), bf16),
                pltpu.VMEM((n_seq, block // 256, MINE, 256), bf16),
                pltpu.VMEM((n_chan, n_seq, MINE, LANES), bf16),
                pltpu.VMEM((model, LANES), bf16),
                sems((8,)),
                sems((4,)),
            ]
            + [sems((n_seq,))] * 8
            + [sems, sems, pltpu.SemaphoreType.REGULAR],
            compiler_params=pltpu.CompilerParams(
                collective_id=0, has_side_effects=True, vmem_limit_bytes=48 * 1024 * 1024
            ),
        )(
            values,
            gate_acts,
            cotangent,
            filter_taps,
            jnp.asarray(high),
            jnp.asarray(low),
            w_value,
            w_gate,
        )

    return jax.shard_map(
        local,
        mesh=mesh,
        in_specs=(P("chan", "seq"), P("chan", "seq"), P("chan", "seq"), P("chan", "seq"), P(), P()),
        out_specs=(P(("seq", "chan"), None), P("chan", "seq")),
        check_vma=False,
    )
```

```python
import functools

import numpy as np

import jax
import jax.numpy as jnp
import ml_dtypes
from jax import lax
from jax.experimental import pallas as pl
from jax.experimental.pallas import tpu as pltpu
from jax.sharding import PartitionSpec as P

MESH = pl.DeviceIdType.MESH
LANES = 128
MINE = 4
GROUP = 4
WIDE = 256


def dft_tables(block):
    half = block // 2
    chunks = half // LANES
    order = np.concatenate([np.arange(0, half, 2), np.arange(1, half, 2)])
    token = np.concatenate([np.arange(0, block, 2), np.arange(1, block, 2)])
    steps = (2 * order + 1)[None, :] * token[:, None] % (4 * block)
    angle = np.pi * steps / (2 * block)
    table = np.stack([np.cos(angle), -np.sin(angle)]).reshape(2, block, chunks, LANES)
    table = table.transpose(2, 1, 0, 3).reshape(chunks, block, 2 * LANES)
    high = table.astype(ml_dtypes.bfloat16)
    low = (table - high.astype(np.float64)).astype(ml_dtypes.bfloat16)
    split = (np.arange(block)[:, None] == token[None, :]).astype(ml_dtypes.bfloat16)
    return high, low, split


def kernel(
    n_seq,
    n_chan,
    values_hbm,
    gates_hbm,
    cotangent_hbm,
    taps_hbm,
    high_hbm,
    low_hbm,
    split_hbm,
    wv_hbm,
    wg_hbm,
    input_grad,
    filter_grad,
    values,
    gates,
    cotangent,
    taps,
    high,
    low,
    split,
    wv,
    wg,
    mixed,
    flat,
    send_uv,
    send_h,
    send_c,
    got_uv,
    got_h,
    got_c,
    rows_uv,
    rows_h,
    spec_uv,
    spec_h,
    sums,
    diffs,
    packed_f,
    packed_m,
    signal_f,
    signal_m,
    send_t,
    send_f,
    got_f,
    tiles,
    stacked,
    load_sem,
    own_sem,
    uv_send,
    uv_recv,
    h_send,
    h_recv,
    c_send,
    c_recv,
    f_send,
    f_recv,
    t_send,
    t_recv,
    met,
):
    f32 = jnp.float32
    bf16 = jnp.bfloat16
    me = lax.axis_index("seq")
    my_chan = lax.axis_index("chan")
    block = values.shape[1]
    half = block // 2
    chunks = half // LANES
    share = block // n_chan
    pairs = n_seq // 2

    loads = [
        pltpu.make_async_copy(src, dst, load_sem.at[i])
        for i, (src, dst) in enumerate(
            (
                (taps_hbm, taps),
                (values_hbm, values),
                (gates_hbm, gates),
                (cotangent_hbm, cotangent),
                (split_hbm, split),
                (high_hbm, high),
                (low_hbm, low),
                (wv_hbm, wv),
                (wg_hbm, wg),
            )
        )
    ]
    for load in loads:
        load.start()

    barrier = pltpu.get_barrier_semaphore()

    def greet_seq(k, carry):
        pl.semaphore_signal(
            barrier, inc=1, device_id={"seq": me ^ k}, device_id_type=MESH
        )
        return carry

    def greet_chan(k, carry):
        pl.semaphore_signal(
            barrier, inc=1, device_id={"chan": my_chan ^ k}, device_id_type=MESH
        )
        return carry

    lax.fori_loop(1, n_seq, greet_seq, 0)
    lax.fori_loop(1, n_chan, greet_chan, 0)

    for load in loads[:4]:
        load.wait()
    channels = values.shape[0]
    mixed[0:channels, :] = taps[...].astype(bf16)
    mixed[channels : 2 * channels, :] = values[...]
    cot = cotangent[...]
    upstream = cot.astype(f32) * gates[...].astype(f32)
    mixed[2 * channels : 3 * channels, :] = upstream.astype(bf16)
    mixed[3 * channels : 4 * channels, :] = cot
    loads[4].wait()

    def divide(t, carry):
        at = pl.ds(pl.multiple_of(t * WIDE, WIDE), WIDE)
        flat[:, at] = jnp.dot(mixed[...], split[:, at], preferred_element_type=f32)
        return carry

    lax.fori_loop(0, block // WIDE, divide, 0)

    def pack(t, carry):
        h, v, u, c = (
            flat[pl.ds(pl.multiple_of(i * channels + t * 8, 8), 8), :] for i in range(4)
        )
        for side in range(2):
            part = slice(side * MINE, side * MINE + MINE)
            uv = jnp.concatenate([u[part], v[part]], 0)
            send_uv[2 * t + side] = uv.astype(bf16)
            send_h[2 * t + side] = h[part].astype(bf16)
            send_c[2 * t + side] = c[part].astype(bf16)
        return carry

    lax.fori_loop(0, pairs, pack, 0)
    pl.semaphore_wait(barrier, n_seq + n_chan - 2)

    def pair_of(i):
        return (me // 2) ^ (2 * (i % (pairs // 2)) + 1 - i // (pairs // 2))

    def to_seq(src, dst, send_sem, recv_sem, peer, slot):
        return pltpu.make_async_remote_copy(
            src_ref=src.at[peer],
            dst_ref=dst.at[slot],
            send_sem=send_sem.at[peer],
            recv_sem=recv_sem.at[slot],
            device_id={"seq": peer},
            device_id_type=MESH,
        )

    def send_all(src, dst, send_sem, recv_sem):
        def step(i, carry):
            for side in range(2):
                peer = 2 * pair_of(i) + side

                @pl.when(peer != me)
                def _():
                    to_seq(src, dst, send_sem, recv_sem, peer, me).start()

            return carry

        lax.fori_loop(0, pairs, step, 0)

    def wait_all(src, dst, send_sem, recv_sem):
        def step(k, carry):
            copy = to_seq(src, dst, send_sem, recv_sem, me ^ k, me ^ k)
            copy.wait_send()
            copy.wait_recv()
            return carry

        lax.fori_loop(1, n_seq, step, 0)

    send_all(send_uv, got_uv, uv_send, uv_recv)
    send_all(send_h, got_h, h_send, h_recv)
    send_all(send_c, got_c, c_send, c_recv)
    own = [
        pltpu.make_async_copy(src.at[me], dst.at[me], own_sem.at[i])
        for i, (src, dst) in enumerate(
            ((send_uv, got_uv), (send_h, got_h), (send_c, got_c))
        )
    ]
    for copy in own:
        copy.start()

    def met_chan(k, carry):
        pl.semaphore_signal(met, inc=1, device_id={"chan": my_chan ^ k}, device_id_type=MESH)
        return carry

    lax.fori_loop(1, n_chan, met_chan, 0)
    loads[5].wait()
    loads[6].wait()
    own[0].wait()
    wait_all(send_uv, got_uv, uv_send, uv_recv)

    flip = jnp.where(
        lax.broadcasted_iota(jnp.int32, (MINE, block), 1) < half, 1.0, -1.0
    ).astype(f32)

    def build_uv(t, carry):
        pair = [got_uv[2 * t + i].astype(f32) for i in range(2)]
        for n, part in enumerate((slice(0, MINE), slice(MINE, 2 * MINE))):
            x, y = pair[0][part], pair[1][part]
            tile = jnp.concatenate([x, x * flip, y, y * flip], 0)
            at = pl.ds(pl.multiple_of(n * n_seq * 8 + t * 16, 16), 16)
            rows_uv[at, :] = tile.astype(bf16)
        return carry

    lax.fori_loop(0, pairs, build_uv, 0)

    re = slice(0, LANES)
    im = slice(LANES, 2 * LANES)
    turn = (((1,), (1,)), ((), ()))
    upper = lax.broadcasted_iota(jnp.int32, (8, LANES), 0) < MINE
    scale = 1.0 / (block * 128.0)

    def times_table(lhs, j):
        return jnp.dot(lhs, high[j], preferred_element_type=f32) + jnp.dot(
            lhs, low[j], preferred_element_type=f32
        )

    def add(acc, term):
        return term if acc is None else (acc[0] + term[0], acc[1] + term[1])

    def fold(base, done, offset):
        for i in range(0, GROUP, 2):
            at = slice(offset + (base + i) * MINE, offset + (base + i) * MINE + 8)
            for lane, part in ((re, 0), (im, 1)):
                x, y = done[i][part], done[i + 1][part]
                rx, ry = pltpu.roll(x, MINE, axis=0), pltpu.roll(y, MINE, axis=0)
                sums[at, lane] = jnp.where(upper, x + rx, y + ry)
                diffs[at, lane] = jnp.where(upper, x - rx, ry - y)

    def correlate(p, q, sign, offset):
        after = None
        for base in reversed(range(0, n_seq, GROUP)):
            acc = [None] * GROUP
            for c in range(n_seq - base):
                pr, pi = p(c)
                for i in range(GROUP):
                    if base + i + c < n_seq:
                        qr, qi = q(base + i + c)
                        acc[i] = add(acc[i], (pr * qr + pi * qi, pr * qi - pi * qr))
            done = [None] * GROUP
            for i in reversed(range(GROUP)):
                zr, zi = acc[i]
                if after is None:
                    done[i] = (zr, zi)
                else:
                    done[i] = (zr + sign * after[1], zi - sign * after[0])
                after = (zr, zi)
            fold(base, done, offset)

    def convolve(p, q, sign, offset):
        before = None
        for base in range(0, n_seq, GROUP):
            acc = [None] * GROUP
            for c in range(base + GROUP):
                pr, pi = p(c)
                for i in range(GROUP):
                    if base + i - c >= 0:
                        qr, qi = q(base + i - c)
                        acc[i] = add(acc[i], (pr * qr - pi * qi, pr * qi + pi * qr))
            done = [None] * GROUP
            for i in range(GROUP):
                zr, zi = acc[i]
                if before is None:
                    done[i] = (zr, zi)
                else:
                    done[i] = (zr - sign * before[1], zi + sign * before[0])
                before = (zr, zi)
            fold(base, done, offset)

    def upstream_of(j):
        def tile(a):
            at = slice(a * 8, a * 8 + 8)
            return spec_uv[j, at, re], spec_uv[j, at, im]

        return tile

    def value_of(j):
        def tile(a):
            at = slice((n_seq + a) * 8, (n_seq + a) * 8 + 8)
            return spec_uv[j, at, re], spec_uv[j, at, im]

        return tile

    def tap(a):
        at = slice(a * 8, a * 8 + 8)
        return spec_h[at, re], spec_h[at, im]

    def sign_of(j):
        return jnp.where(j < chunks // 2, 1.0, -1.0).astype(f32)

    small = n_seq * MINE

    def first_spectra(j, carry):
        spec_uv[j] = times_table(rows_uv[...], j)
        correlate(value_of(j), upstream_of(j), sign_of(j), 0)
        packed_f[0, j] = sums[:small, :].astype(bf16)
        packed_f[1, j] = diffs[:small, :].astype(bf16)
        return carry

    lax.fori_loop(0, chunks, first_spectra, 0)

    def back(packed, parity, start):
        total = None
        at = pl.ds(pl.multiple_of(parity * half + start, WIDE), WIDE)
        for j in range(chunks):
            lhs = packed[parity, j]
            part = lax.dot_general(lhs, high[j, at, :], turn, preferred_element_type=f32)
            part = part + lax.dot_general(
                lhs, low[j, at, :], turn, preferred_element_type=f32
            )
            total = part if total is None else total + part
        return total * scale

    def inverse_f(t, carry):
        for parity in range(2):
            at = pl.ds(pl.multiple_of(parity * half + t * WIDE, WIDE), WIDE)
            signal_f[:, at] = back(packed_f, parity, t * WIDE).astype(bf16)
        return carry

    lax.fori_loop(0, half // WIDE, inverse_f, 0)

    def join(t, carry):
        at = pl.ds(pl.multiple_of(t * WIDE, WIDE), WIDE)
        whole = lax.dot_general(
            signal_f[...], split[at, :], turn, preferred_element_type=f32
        )
        for a in range(n_seq):
            send_f[a, t] = whole[a * MINE : a * MINE + MINE].astype(bf16)
        return carry

    lax.fori_loop(0, block // WIDE, join, 0)
    own_f = pltpu.make_async_copy(send_f.at[me], got_f.at[me], own_sem.at[3])
    own_f.start()
    send_all(send_f, got_f, f_send, f_recv)

    own[1].wait()
    wait_all(send_h, got_h, h_send, h_recv)

    def build_h(t, carry):
        x, y = (got_h[2 * t + i].astype(f32) for i in range(2))
        tile = jnp.concatenate([x, x * flip, y, y * flip], 0)
        rows_h[pl.ds(pl.multiple_of(t * 16, 16), 16), :] = tile.astype(bf16)
        return carry

    lax.fori_loop(0, pairs, build_h, 0)

    def second_spectra(j, carry):
        spec_h[...] = times_table(rows_h[...], j)
        correlate(tap, upstream_of(j), sign_of(j), 0)
        convolve(tap, value_of(j), sign_of(j), small)
        packed_m[0, j] = sums[...].astype(bf16)
        packed_m[1, j] = diffs[...].astype(bf16)
        return carry

    lax.fori_loop(0, chunks, second_spectra, 0)

    own[2].wait()
    wait_all(send_c, got_c, c_send, c_recv)
    pl.semaphore_wait(met, n_chan - 1)

    piece = share // 2
    lane_piece = lax.broadcasted_iota(jnp.int32, (8, LANES), 1) // piece
    per_tile = LANES // piece

    def to_owner(a, c):
        return pltpu.make_async_remote_copy(
            src_ref=send_t.at[a, c],
            dst_ref=tiles.at[my_chan, me],
            send_sem=t_send,
            recv_sem=t_recv,
            device_id={"seq": a, "chan": c},
            device_id_type=MESH,
        )

    def inverse_m(t, carry):
        for parity in range(2):
            signal_m[parity] = back(packed_m, parity, t * WIDE)

        def finish(i, carry):
            pair = pair_of(i)
            at_v = pl.ds(pl.multiple_of(pair * 8, 8), 8)
            at_c = pl.ds(pl.multiple_of(small + pair * 8, 8), 8)
            parts = [signal_m[parity, at_v, :] for parity in range(2)]
            for parity in range(2):
                at = pl.ds(pl.multiple_of(parity * half + t * WIDE, WIDE), WIDE)
                cots = jnp.concatenate(
                    [got_c[2 * pair + side, :, at].astype(f32) for side in range(2)], 0
                )
                parts.append(signal_m[parity, at_c, :] * cots)
            for p in range(WIDE // LANES):
                lane = slice(p * LANES, (p + 1) * LANES)
                moved = [parts[0][:, lane]] + [
                    pltpu.roll(parts[n][:, lane], n * piece, axis=1) for n in range(1, 4)
                ]
                for q in range(per_tile):
                    out = moved[0]
                    for n in range(1, 4):
                        out = jnp.where(lane_piece == (q + n) % 4, moved[n], out)
                    c = (t * (WIDE // LANES) + p) * per_tile + q
                    for side in range(2):
                        part = out[side * MINE : side * MINE + MINE]
                        send_t[2 * pair + side, c] = part.astype(bf16)
            for q in range(WIDE // piece):
                c = t * (WIDE // piece) + q
                for side in range(2):
                    a = 2 * pair + side

                    @pl.when((a != me) | (c != my_chan))
                    def _():
                        to_owner(a, c).start()

            return carry

        lax.fori_loop(0, pairs, finish, 0)
        return carry

    lax.fori_loop(0, half // WIDE, inverse_m, 0)
    own_t = pltpu.make_async_copy(send_t.at[me, my_chan], tiles.at[my_chan, me], t_recv)
    own_t.start()

    own_f.wait()
    wait_all(send_f, got_f, f_send, f_recv)

    def unpack(i, carry):
        at = pl.ds(pl.multiple_of(i * 8, 8), 8)
        for t in range(block // WIDE):
            pair = [got_f[2 * i + side, t].astype(f32) for side in range(2)]
            filter_grad[at, t * WIDE : (t + 1) * WIDE] = jnp.concatenate(pair, 0)
        return carry

    lax.fori_loop(0, pairs, unpack, 0)
    loads[7].wait()
    loads[8].wait()

    pltpu.make_async_copy(tiles, tiles, t_recv).wait()

    def restack(c, carry):
        for q in range(n_seq // 4):
            tile = jnp.concatenate(
                [tiles[c, 4 * q + i].astype(f32) for i in range(4)], 0
            )
            at = pl.ds(pl.multiple_of(c * 64 + q * 16, 16), 16)
            stacked[at, :] = tile.astype(bf16)
        return carry

    lax.fori_loop(0, n_chan, restack, 0)

    lane_of = lax.broadcasted_iota(jnp.int32, (LANES, LANES), 1)
    row_of = lax.broadcasted_iota(jnp.int32, (LANES, LANES), 0)
    source = (lane_of // piece + 4 - my_chan % 4) % 4
    wanted = (source // 2) * share + 2 * (lane_of % piece) + source % 2
    choice = jnp.where(row_of == wanted, 1.0, 0.0).astype(bf16)
    tokens = lax.dot_general(choice, stacked[...], turn, preferred_element_type=f32)
    tokens = tokens.astype(bf16)
    out = lax.dot_general(tokens[:share], wv[...], turn, preferred_element_type=f32)
    out = out + lax.dot_general(tokens[share:], wg[...], turn, preferred_element_type=f32)
    input_grad[...] = out.astype(bf16)

    def drain(k, carry):
        pltpu.make_async_copy(send_t.at[k], send_t.at[k], t_send).wait()
        return carry

    lax.fori_loop(1, n_seq, drain, 0)
    rest = send_t.at[0, pl.ds(0, n_chan - 1)]
    pltpu.make_async_copy(rest, rest, t_send).wait()


def solution(mesh):
    n_seq = mesh.shape["seq"]
    n_chan = mesh.shape["chan"]
    bf16 = jnp.bfloat16
    f32 = jnp.float32

    def local(values, gate_acts, cotangent, filter_taps, w_value, w_gate):
        channels, block = values.shape
        chunks = block // 2 // LANES
        model = w_value.shape[0]
        high, low, split = dft_tables(block)
        vmem = pl.BlockSpec(memory_space=pltpu.VMEM)
        hbm = pl.BlockSpec(memory_space=pltpu.MemorySpace.HBM)
        sems = pltpu.SemaphoreType.DMA
        return pl.pallas_call(
            functools.partial(kernel, n_seq, n_chan),
            out_shape=(
                jax.ShapeDtypeStruct((block // n_chan, model), bf16),
                jax.ShapeDtypeStruct((channels, block), f32),
            ),
            in_specs=[hbm] * 9,
            out_specs=(vmem, vmem),
            scratch_shapes=[
                pltpu.VMEM((channels, block), bf16),
                pltpu.VMEM((channels, block), bf16),
                pltpu.VMEM((channels, block), bf16),
                pltpu.VMEM((channels, block), f32),
                pltpu.VMEM((chunks, block, 2 * LANES), bf16),
                pltpu.VMEM((chunks, block, 2 * LANES), bf16),
                pltpu.VMEM((block, block), bf16),
                pltpu.VMEM((model, model), bf16),
                pltpu.VMEM((model, model), bf16),
                pltpu.VMEM((4 * channels, block), bf16),
                pltpu.VMEM((4 * channels, block), f32),
                pltpu.VMEM((n_seq, 2 * MINE, block), bf16),
                pltpu.VMEM((n_seq, MINE, block), bf16),
                pltpu.VMEM((n_seq, MINE, block), bf16),
                pltpu.VMEM((n_seq, 2 * MINE, block), bf16),
                pltpu.VMEM((n_seq, MINE, block), bf16),
                pltpu.VMEM((n_seq, MINE, block), bf16),
                pltpu.VMEM((n_seq * 16, block), bf16),
                pltpu.VMEM((n_seq * 8, block), bf16),
                pltpu.VMEM((chunks, n_seq * 16, 2 * LANES), f32),
                pltpu.VMEM((n_seq * 8, 2 * LANES), f32),
                pltpu.VMEM((n_seq * 8, 2 * LANES), f32),
                pltpu.VMEM((n_seq * 8, 2 * LANES), f32),
                pltpu.VMEM((2, chunks, n_seq * 4, 2 * LANES), bf16),
                pltpu.VMEM((2, chunks, n_seq * 8, 2 * LANES), bf16),
                pltpu.VMEM((n_seq * 4, block), bf16),
                pltpu.VMEM((2, n_seq * 8, WIDE), f32),
                pltpu.VMEM((n_seq, n_chan, MINE, LANES), bf16),
                pltpu.VMEM((n_seq, block // WIDE, MINE, WIDE), bf16),
                pltpu.VMEM((n_seq, block // WIDE, MINE, WIDE), bf16),
                pltpu.VMEM((n_chan, n_seq, MINE, LANES), bf16),
                pltpu.VMEM((model, LANES), bf16),
                sems((9,)),
                sems((4,)),
            ]
            + [sems((n_seq,))] * 8
            + [sems, sems, pltpu.SemaphoreType.REGULAR],
            compiler_params=pltpu.CompilerParams(
                collective_id=0, has_side_effects=True, vmem_limit_bytes=67_043_328
            ),
        )(
            values,
            gate_acts,
            cotangent,
            filter_taps,
            jnp.asarray(high),
            jnp.asarray(low),
            jnp.asarray(split),
            w_value,
            w_gate,
        )

    return jax.shard_map(
        local,
        mesh=mesh,
        in_specs=(P("chan", "seq"), P("chan", "seq"), P("chan", "seq"), P("chan", "seq"), P(), P()),
        out_specs=(P(("seq", "chan"), None), P("chan", "seq")),
        check_vma=False,
    )
```

```python
import functools

import numpy as np

import jax
import jax.numpy as jnp
import ml_dtypes
from jax import lax
from jax.experimental import pallas as pl
from jax.experimental.pallas import tpu as pltpu
from jax.sharding import PartitionSpec as P

MESH = pl.DeviceIdType.MESH
LANES = 128
MINE = 4
GROUP = 4
WIDE = 256


def dft_tables(block):
    half = block // 2
    chunks = half // LANES
    order = np.concatenate([np.arange(0, half, 2), np.arange(1, half, 2)])
    token = np.concatenate([np.arange(0, block, 2), np.arange(1, block, 2)])
    steps = (2 * order + 1)[None, :] * token[:, None] % (4 * block)
    angle = np.pi * steps / (2 * block)
    table = np.stack([np.cos(angle), -np.sin(angle)]).reshape(2, block, chunks, LANES)
    table = table.transpose(2, 1, 0, 3).reshape(chunks, block, 2 * LANES)
    high = table.astype(ml_dtypes.bfloat16)
    low = (table - high.astype(np.float64)).astype(ml_dtypes.bfloat16)
    split = (np.arange(block)[:, None] == token[None, :]).astype(ml_dtypes.bfloat16)
    return high, low, split


def kernel(
    n_seq,
    n_chan,
    values_hbm,
    gates_hbm,
    cotangent_hbm,
    taps_hbm,
    high_hbm,
    low_hbm,
    split_hbm,
    wv_hbm,
    wg_hbm,
    input_grad,
    filter_grad,
    values,
    gates,
    cotangent,
    taps,
    high,
    low,
    split,
    wv,
    wg,
    mixed,
    flat,
    send_uv,
    send_h,
    send_c,
    got_uv,
    got_h,
    got_c,
    rows_uv,
    rows_h,
    spec_uv,
    spec_h,
    sums,
    diffs,
    packed_f,
    packed_m,
    signal_f,
    signal_m,
    send_t,
    send_f,
    got_f,
    tiles,
    stacked,
    load_sem,
    own_sem,
    uv_send,
    uv_recv,
    h_send,
    h_recv,
    c_send,
    c_recv,
    f_send,
    f_recv,
    t_send,
    t_recv,
    met,
):
    f32 = jnp.float32
    bf16 = jnp.bfloat16
    me = lax.axis_index("seq")
    my_chan = lax.axis_index("chan")
    block = values.shape[1]
    half = block // 2
    chunks = half // LANES
    share = block // n_chan
    pairs = n_seq // 2

    loads = [
        pltpu.make_async_copy(src, dst, load_sem.at[i])
        for i, (src, dst) in enumerate(
            (
                (taps_hbm, taps),
                (values_hbm, values),
                (gates_hbm, gates),
                (cotangent_hbm, cotangent),
                (split_hbm, split),
                (high_hbm, high),
                (low_hbm, low),
                (wv_hbm, wv),
                (wg_hbm, wg),
            )
        )
    ]
    for load in loads:
        load.start()

    barrier = pltpu.get_barrier_semaphore()

    def greet_seq(k, carry):
        pl.semaphore_signal(
            barrier, inc=1, device_id={"seq": me ^ k}, device_id_type=MESH
        )
        return carry

    def greet_chan(k, carry):
        pl.semaphore_signal(
            barrier, inc=1, device_id={"chan": my_chan ^ k}, device_id_type=MESH
        )
        return carry

    lax.fori_loop(1, n_seq, greet_seq, 0)
    lax.fori_loop(1, n_chan, greet_chan, 0)

    for load in loads[:4]:
        load.wait()
    channels = values.shape[0]
    mixed[0:channels, :] = taps[...].astype(bf16)
    mixed[channels : 2 * channels, :] = values[...]
    cot = cotangent[...]
    upstream = cot.astype(f32) * gates[...].astype(f32)
    mixed[2 * channels : 3 * channels, :] = upstream.astype(bf16)
    mixed[3 * channels : 4 * channels, :] = cot
    loads[4].wait()

    def divide(t, carry):
        at = pl.ds(pl.multiple_of(t * WIDE, WIDE), WIDE)
        flat[:, at] = jnp.dot(mixed[...], split[:, at], preferred_element_type=f32)
        return carry

    lax.fori_loop(0, block // WIDE, divide, 0)

    def pack(t, carry):
        h, v, u, c = (
            flat[pl.ds(pl.multiple_of(i * channels + t * 8, 8), 8), :] for i in range(4)
        )
        for side in range(2):
            part = slice(side * MINE, side * MINE + MINE)
            uv = jnp.concatenate([u[part], v[part]], 0)
            send_uv[2 * t + side] = uv.astype(bf16)
            send_h[2 * t + side] = h[part].astype(bf16)
            send_c[2 * t + side] = c[part].astype(bf16)
        return carry

    lax.fori_loop(0, pairs, pack, 0)
    pl.semaphore_wait(barrier, n_seq + n_chan - 2)

    def pair_of(i):
        return (me // 2) ^ (2 * (i % (pairs // 2)) + 1 - i // (pairs // 2))

    def to_seq(src, dst, send_sem, recv_sem, peer, slot):
        return pltpu.make_async_remote_copy(
            src_ref=src.at[peer],
            dst_ref=dst.at[slot],
            send_sem=send_sem.at[peer],
            recv_sem=recv_sem.at[slot],
            device_id={"seq": peer},
            device_id_type=MESH,
        )

    def send_all(src, dst, send_sem, recv_sem):
        def step(i, carry):
            for side in range(2):
                peer = 2 * pair_of(i) + side

                @pl.when(peer != me)
                def _():
                    to_seq(src, dst, send_sem, recv_sem, peer, me).start()

            return carry

        lax.fori_loop(0, pairs, step, 0)

    def wait_all(src, dst, send_sem, recv_sem):
        def step(k, carry):
            copy = to_seq(src, dst, send_sem, recv_sem, me ^ k, me ^ k)
            copy.wait_send()
            copy.wait_recv()
            return carry

        lax.fori_loop(1, n_seq, step, 0)

    send_all(send_uv, got_uv, uv_send, uv_recv)
    send_all(send_h, got_h, h_send, h_recv)
    send_all(send_c, got_c, c_send, c_recv)
    own = [
        pltpu.make_async_copy(src.at[me], dst.at[me], own_sem.at[i])
        for i, (src, dst) in enumerate(
            ((send_uv, got_uv), (send_h, got_h), (send_c, got_c))
        )
    ]
    for copy in own:
        copy.start()

    def met_chan(k, carry):
        pl.semaphore_signal(met, inc=1, device_id={"chan": my_chan ^ k}, device_id_type=MESH)
        return carry

    lax.fori_loop(1, n_chan, met_chan, 0)
    loads[5].wait()
    loads[6].wait()
    own[0].wait()
    wait_all(send_uv, got_uv, uv_send, uv_recv)

    flip = jnp.where(
        lax.broadcasted_iota(jnp.int32, (MINE, block), 1) < half, 1.0, -1.0
    ).astype(f32)

    def build_uv(t, carry):
        pair = [got_uv[2 * t + i].astype(f32) for i in range(2)]
        for n, part in enumerate((slice(0, MINE), slice(MINE, 2 * MINE))):
            x, y = pair[0][part], pair[1][part]
            tile = jnp.concatenate([x, x * flip, y, y * flip], 0)
            at = pl.ds(pl.multiple_of(n * n_seq * 8 + t * 16, 16), 16)
            rows_uv[at, :] = tile.astype(bf16)
        return carry

    lax.fori_loop(0, pairs, build_uv, 0)

    re = slice(0, LANES)
    im = slice(LANES, 2 * LANES)
    turn = (((1,), (1,)), ((), ()))
    upper = lax.broadcasted_iota(jnp.int32, (8, LANES), 0) < MINE
    scale = 1.0 / (block * 128.0)

    def times_table(lhs, j):
        return jnp.dot(lhs, high[j], preferred_element_type=f32) + jnp.dot(
            lhs, low[j], preferred_element_type=f32
        )

    def add(acc, term):
        return term if acc is None else (acc[0] + term[0], acc[1] + term[1])

    def fold(base, done, j, offset):
        for i in range(0, GROUP, 2):
            at = slice(offset + (base + i) * MINE, offset + (base + i) * MINE + 8)
            for lane, part in ((re, 0), (im, 1)):
                x, y = done[i][part], done[i + 1][part]
                rx, ry = pltpu.roll(x, MINE, axis=0), pltpu.roll(y, MINE, axis=0)
                sums[j, at, lane] = jnp.where(upper, x + rx, y + ry)
                diffs[j, at, lane] = jnp.where(upper, x - rx, ry - y)

    def correlate(p, q, sign, j, offset):
        after = None
        for base in reversed(range(0, n_seq, GROUP)):
            acc = [None] * GROUP
            for c in range(n_seq - base):
                pr, pi = p(c)
                for i in range(GROUP):
                    if base + i + c < n_seq:
                        qr, qi = q(base + i + c)
                        acc[i] = add(acc[i], (pr * qr + pi * qi, pr * qi - pi * qr))
            done = [None] * GROUP
            for i in reversed(range(GROUP)):
                zr, zi = acc[i]
                if after is None:
                    done[i] = (zr, zi)
                else:
                    done[i] = (zr + sign * after[1], zi - sign * after[0])
                after = (zr, zi)
            fold(base, done, j, offset)

    def convolve(p, q, sign, j, offset):
        before = None
        for base in range(0, n_seq, GROUP):
            acc = [None] * GROUP
            for c in range(base + GROUP):
                pr, pi = p(c)
                for i in range(GROUP):
                    if base + i - c >= 0:
                        qr, qi = q(base + i - c)
                        acc[i] = add(acc[i], (pr * qr - pi * qi, pr * qi + pi * qr))
            done = [None] * GROUP
            for i in range(GROUP):
                zr, zi = acc[i]
                if before is None:
                    done[i] = (zr, zi)
                else:
                    done[i] = (zr - sign * before[1], zi + sign * before[0])
                before = (zr, zi)
            fold(base, done, j, offset)

    def upstream_of(j):
        def tile(a):
            at = slice(a * 8, a * 8 + 8)
            return spec_uv[j, at, re], spec_uv[j, at, im]

        return tile

    def value_of(j):
        def tile(a):
            at = slice((n_seq + a) * 8, (n_seq + a) * 8 + 8)
            return spec_uv[j, at, re], spec_uv[j, at, im]

        return tile

    def tap_of(j):
        def tile(a):
            at = slice(a * 8, a * 8 + 8)
            return spec_h[j, at, re], spec_h[j, at, im]

        return tile

    def sign_of(j):
        return jnp.where(j < chunks // 2, 1.0, -1.0).astype(f32)

    small = n_seq * MINE

    def first_spectra(j, carry):
        spec_uv[j] = times_table(rows_uv[...], j)
        correlate(value_of(j), upstream_of(j), sign_of(j), j, 0)
        packed_f[0, j] = sums[j, :small, :].astype(bf16)
        packed_f[1, j] = diffs[j, :small, :].astype(bf16)
        return carry

    lax.fori_loop(0, chunks, first_spectra, 0)

    def back(packed, parity, start, tables):
        total = None
        at = pl.ds(pl.multiple_of(parity * half + start, WIDE), WIDE)
        for j in range(chunks):
            lhs = packed[parity, j]
            for table in tables:
                part = lax.dot_general(
                    lhs, table[j, at, :], turn, preferred_element_type=f32
                )
                total = part if total is None else total + part
        return total * scale

    def inverse_f(t, carry):
        for parity in range(2):
            grads = back(packed_f, parity, t * WIDE, (high,))
            for a in range(n_seq):
                part = grads[a * MINE : a * MINE + MINE]
                send_f[a, parity * (half // WIDE) + t] = part.astype(bf16)
        return carry

    lax.fori_loop(0, half // WIDE, inverse_f, 0)
    own_f = pltpu.make_async_copy(send_f.at[me], got_f.at[me], own_sem.at[3])
    own_f.start()
    send_all(send_f, got_f, f_send, f_recv)

    own[1].wait()
    wait_all(send_h, got_h, h_send, h_recv)

    def build_h(t, carry):
        x, y = (got_h[2 * t + i].astype(f32) for i in range(2))
        tile = jnp.concatenate([x, x * flip, y, y * flip], 0)
        rows_h[pl.ds(pl.multiple_of(t * 16, 16), 16), :] = tile.astype(bf16)
        return carry

    lax.fori_loop(0, pairs, build_h, 0)

    spec_h[0] = times_table(rows_h[...], 0)
    for j in range(chunks):
        if j + 1 < chunks:
            spec_h[j + 1] = times_table(rows_h[...], j + 1)
        correlate(tap_of(j), upstream_of(j), 1.0 if j < chunks // 2 else -1.0, j, 0)
        convolve(tap_of(j), value_of(j), 1.0 if j < chunks // 2 else -1.0, j, small)
        packed_m[0, j] = sums[j].astype(bf16)
        packed_m[1, j] = diffs[j].astype(bf16)

    own[2].wait()
    wait_all(send_c, got_c, c_send, c_recv)
    pl.semaphore_wait(met, n_chan - 1)

    piece = share // 2
    lane_piece = lax.broadcasted_iota(jnp.int32, (8, LANES), 1) // piece
    per_tile = LANES // piece

    def to_owner(a, c):
        return pltpu.make_async_remote_copy(
            src_ref=send_t.at[a, c],
            dst_ref=tiles.at[my_chan, me],
            send_sem=t_send,
            recv_sem=t_recv,
            device_id={"seq": a, "chan": c},
            device_id_type=MESH,
        )

    def inverse_m(t, carry):
        for parity in range(2):
            signal_m[parity] = back(packed_m, parity, t * WIDE, (high, low))

        def finish(i, carry):
            pair = pair_of(i)
            at_v = pl.ds(pl.multiple_of(pair * 8, 8), 8)
            at_c = pl.ds(pl.multiple_of(small + pair * 8, 8), 8)
            parts = [signal_m[parity, at_v, :] for parity in range(2)]
            for parity in range(2):
                at = pl.ds(pl.multiple_of(parity * half + t * WIDE, WIDE), WIDE)
                cots = jnp.concatenate(
                    [got_c[2 * pair + side, :, at].astype(f32) for side in range(2)], 0
                )
                parts.append(signal_m[parity, at_c, :] * cots)
            for p in range(WIDE // LANES):
                lane = slice(p * LANES, (p + 1) * LANES)
                moved = [parts[0][:, lane]] + [
                    pltpu.roll(parts[n][:, lane], n * piece, axis=1) for n in range(1, 4)
                ]
                for q in range(per_tile):
                    out = moved[0]
                    for n in range(1, 4):
                        out = jnp.where(lane_piece == (q + n) % 4, moved[n], out)
                    c = (t * (WIDE // LANES) + p) * per_tile + q
                    for side in range(2):
                        part = out[side * MINE : side * MINE + MINE]
                        send_t[2 * pair + side, c] = part.astype(bf16)
            for q in range(WIDE // piece):
                c = t * (WIDE // piece) + q
                for side in range(2):
                    a = 2 * pair + side

                    @pl.when((a != me) | (c != my_chan))
                    def _():
                        to_owner(a, c).start()

            return carry

        lax.fori_loop(0, pairs, finish, 0)
        return carry

    lax.fori_loop(0, half // WIDE, inverse_m, 0)
    own_t = pltpu.make_async_copy(send_t.at[me, my_chan], tiles.at[my_chan, me], t_recv)
    own_t.start()

    own_f.wait()
    wait_all(send_f, got_f, f_send, f_recv)

    def unpack(i, carry):
        at = pl.ds(pl.multiple_of(i * 16, 16), 16)
        for t in range(block // WIDE):
            tile = [got_f[4 * i + n, t].astype(f32) for n in range(4)]
            lane = slice(t * WIDE, (t + 1) * WIDE)
            signal_f[at, lane] = jnp.concatenate(tile, 0).astype(bf16)
        return carry

    lax.fori_loop(0, n_seq // 4, unpack, 0)

    def join(t, carry):
        at = pl.ds(pl.multiple_of(t * WIDE, WIDE), WIDE)
        filter_grad[:, at] = lax.dot_general(
            signal_f[...], split[at, :], turn, preferred_element_type=f32
        )
        return carry

    lax.fori_loop(0, block // WIDE, join, 0)
    loads[7].wait()
    loads[8].wait()

    pltpu.make_async_copy(tiles, tiles, t_recv).wait()

    def restack(c, carry):
        for q in range(n_seq // 4):
            tile = jnp.concatenate(
                [tiles[c, 4 * q + i].astype(f32) for i in range(4)], 0
            )
            at = pl.ds(pl.multiple_of(c * 64 + q * 16, 16), 16)
            stacked[at, :] = tile.astype(bf16)
        return carry

    lax.fori_loop(0, n_chan, restack, 0)

    lane_of = lax.broadcasted_iota(jnp.int32, (LANES, LANES), 1)
    row_of = lax.broadcasted_iota(jnp.int32, (LANES, LANES), 0)
    source = (lane_of // piece + 4 - my_chan % 4) % 4
    wanted = (source // 2) * share + 2 * (lane_of % piece) + source % 2
    choice = jnp.where(row_of == wanted, 1.0, 0.0).astype(bf16)
    tokens = lax.dot_general(choice, stacked[...], turn, preferred_element_type=f32)
    tokens = tokens.astype(bf16)
    out = lax.dot_general(tokens[:share], wv[...], turn, preferred_element_type=f32)
    out = out + lax.dot_general(tokens[share:], wg[...], turn, preferred_element_type=f32)
    input_grad[...] = out.astype(bf16)

    def drain(k, carry):
        pltpu.make_async_copy(send_t.at[k], send_t.at[k], t_send).wait()
        return carry

    lax.fori_loop(1, n_seq, drain, 0)
    rest = send_t.at[0, pl.ds(0, n_chan - 1)]
    pltpu.make_async_copy(rest, rest, t_send).wait()


def solution(mesh):
    n_seq = mesh.shape["seq"]
    n_chan = mesh.shape["chan"]
    bf16 = jnp.bfloat16
    f32 = jnp.float32

    def local(values, gate_acts, cotangent, filter_taps, w_value, w_gate):
        channels, block = values.shape
        chunks = block // 2 // LANES
        model = w_value.shape[0]
        high, low, split = dft_tables(block)
        vmem = pl.BlockSpec(memory_space=pltpu.VMEM)
        hbm = pl.BlockSpec(memory_space=pltpu.MemorySpace.HBM)
        sems = pltpu.SemaphoreType.DMA
        return pl.pallas_call(
            functools.partial(kernel, n_seq, n_chan),
            out_shape=(
                jax.ShapeDtypeStruct((block // n_chan, model), bf16),
                jax.ShapeDtypeStruct((channels, block), f32),
            ),
            in_specs=[hbm] * 9,
            out_specs=(vmem, vmem),
            scratch_shapes=[
                pltpu.VMEM((channels, block), bf16),
                pltpu.VMEM((channels, block), bf16),
                pltpu.VMEM((channels, block), bf16),
                pltpu.VMEM((channels, block), f32),
                pltpu.VMEM((chunks, block, 2 * LANES), bf16),
                pltpu.VMEM((chunks, block, 2 * LANES), bf16),
                pltpu.VMEM((block, block), bf16),
                pltpu.VMEM((model, model), bf16),
                pltpu.VMEM((model, model), bf16),
                pltpu.VMEM((4 * channels, block), bf16),
                pltpu.VMEM((4 * channels, block), f32),
                pltpu.VMEM((n_seq, 2 * MINE, block), bf16),
                pltpu.VMEM((n_seq, MINE, block), bf16),
                pltpu.VMEM((n_seq, MINE, block), bf16),
                pltpu.VMEM((n_seq, 2 * MINE, block), bf16),
                pltpu.VMEM((n_seq, MINE, block), bf16),
                pltpu.VMEM((n_seq, MINE, block), bf16),
                pltpu.VMEM((n_seq * 16, block), bf16),
                pltpu.VMEM((n_seq * 8, block), bf16),
                pltpu.VMEM((chunks, n_seq * 16, 2 * LANES), f32),
                pltpu.VMEM((chunks, n_seq * 8, 2 * LANES), f32),
                pltpu.VMEM((chunks, n_seq * 8, 2 * LANES), f32),
                pltpu.VMEM((chunks, n_seq * 8, 2 * LANES), f32),
                pltpu.VMEM((2, chunks, n_seq * 4, 2 * LANES), bf16),
                pltpu.VMEM((2, chunks, n_seq * 8, 2 * LANES), bf16),
                pltpu.VMEM((n_seq * 4, block), bf16),
                pltpu.VMEM((2, n_seq * 8, WIDE), f32),
                pltpu.VMEM((n_seq, n_chan, MINE, LANES), bf16),
                pltpu.VMEM((n_seq, block // WIDE, MINE, WIDE), bf16),
                pltpu.VMEM((n_seq, block // WIDE, MINE, WIDE), bf16),
                pltpu.VMEM((n_chan, n_seq, MINE, LANES), bf16),
                pltpu.VMEM((model, LANES), bf16),
                sems((9,)),
                sems((4,)),
            ]
            + [sems((n_seq,))] * 8
            + [sems, sems, pltpu.SemaphoreType.REGULAR],
            compiler_params=pltpu.CompilerParams(
                collective_id=0, has_side_effects=True, vmem_limit_bytes=67_043_328
            ),
        )(
            values,
            gate_acts,
            cotangent,
            filter_taps,
            jnp.asarray(high),
            jnp.asarray(low),
            jnp.asarray(split),
            w_value,
            w_gate,
        )

    return jax.shard_map(
        local,
        mesh=mesh,
        in_specs=(P("chan", "seq"), P("chan", "seq"), P("chan", "seq"), P("chan", "seq"), P(), P()),
        out_specs=(P(("seq", "chan"), None), P("chan", "seq")),
        check_vma=False,
    )
```

```python
import functools

import numpy as np

import jax
import jax.numpy as jnp
import ml_dtypes
from jax import lax
from jax.experimental import pallas as pl
from jax.experimental.pallas import tpu as pltpu
from jax.sharding import PartitionSpec as P

MESH = pl.DeviceIdType.MESH
LANES = 128
MINE = 4
GROUP = 4
WIDE = 256


def dft_tables(block):
    half = block // 2
    chunks = half // LANES
    order = np.concatenate([np.arange(0, half, 2), np.arange(1, half, 2)])
    token = np.concatenate([np.arange(0, block, 2), np.arange(1, block, 2)])
    steps = (2 * order + 1)[None, :] * token[:, None] % (4 * block)
    angle = np.pi * steps / (2 * block)
    table = np.stack([np.cos(angle), -np.sin(angle)]).reshape(2, block, chunks, LANES)
    table = table.transpose(2, 1, 0, 3).reshape(chunks, block, 2 * LANES)
    high = table.astype(ml_dtypes.bfloat16)
    low = (table - high.astype(np.float64)).astype(ml_dtypes.bfloat16)
    split = (np.arange(block)[:, None] == token[None, :]).astype(ml_dtypes.bfloat16)
    return high, low, split


def kernel(
    n_seq,
    n_chan,
    values_hbm,
    gates_hbm,
    cotangent_hbm,
    taps_hbm,
    high_hbm,
    low_hbm,
    split_hbm,
    wv_hbm,
    wg_hbm,
    input_grad,
    filter_grad,
    values,
    gates,
    cotangent,
    taps,
    high,
    low,
    split,
    wv,
    wg,
    mixed,
    flat,
    send_u,
    send_v,
    send_h,
    send_c,
    got_u,
    got_v,
    got_h,
    got_c,
    rows_u,
    rows_v,
    rows_h,
    spec_u,
    spec_v,
    spec_h,
    sums,
    diffs,
    packed_f,
    packed_m,
    signal_f,
    signal_m,
    send_t,
    send_f,
    got_f,
    tiles,
    stacked,
    load_sem,
    own_sem,
    u_send,
    u_recv,
    v_send,
    v_recv,
    h_send,
    h_recv,
    c_send,
    c_recv,
    f_send,
    f_recv,
    t_send,
    t_recv,
    met,
):
    f32 = jnp.float32
    bf16 = jnp.bfloat16
    me = lax.axis_index("seq")
    my_chan = lax.axis_index("chan")
    block = values.shape[1]
    half = block // 2
    chunks = half // LANES
    share = block // n_chan
    pairs = n_seq // 2

    loads = [
        pltpu.make_async_copy(src, dst, load_sem.at[i])
        for i, (src, dst) in enumerate(
            (
                (taps_hbm, taps),
                (values_hbm, values),
                (gates_hbm, gates),
                (cotangent_hbm, cotangent),
                (split_hbm, split),
                (high_hbm, high),
                (low_hbm, low),
                (wv_hbm, wv),
                (wg_hbm, wg),
            )
        )
    ]
    for load in loads:
        load.start()

    barrier = pltpu.get_barrier_semaphore()

    def greet_seq(k, carry):
        pl.semaphore_signal(
            barrier, inc=1, device_id={"seq": me ^ k}, device_id_type=MESH
        )
        return carry

    def greet_chan(k, carry):
        pl.semaphore_signal(
            barrier, inc=1, device_id={"chan": my_chan ^ k}, device_id_type=MESH
        )
        return carry

    for k in sorted(range(1, n_seq), key=lambda k: -(k & 2)):
        greet_seq(k, 0)
    lax.fori_loop(1, n_chan, greet_chan, 0)

    for load in loads[:4]:
        load.wait()
    channels = values.shape[0]
    mixed[0:channels, :] = taps[...].astype(bf16)
    mixed[channels : 2 * channels, :] = values[...]
    cot = cotangent[...]
    upstream = cot.astype(f32) * gates[...].astype(f32)
    mixed[2 * channels : 3 * channels, :] = upstream.astype(bf16)
    mixed[3 * channels : 4 * channels, :] = cot
    loads[4].wait()

    def divide(t, carry):
        at = pl.ds(pl.multiple_of(t * WIDE, WIDE), WIDE)
        flat[:, at] = jnp.dot(mixed[...], split[:, at], preferred_element_type=f32)
        return carry

    lax.fori_loop(0, block // WIDE, divide, 0)

    def pack(t, carry):
        h, v, u, c = (
            flat[pl.ds(pl.multiple_of(i * channels + t * 8, 8), 8), :] for i in range(4)
        )
        for side in range(2):
            part = slice(side * MINE, side * MINE + MINE)
            send_u[2 * t + side] = u[part].astype(bf16)
            send_v[2 * t + side] = v[part].astype(bf16)
            send_h[2 * t + side] = h[part].astype(bf16)
            send_c[2 * t + side] = c[part].astype(bf16)
        return carry

    lax.fori_loop(0, pairs, pack, 0)
    pl.semaphore_wait(barrier, n_seq + n_chan - 2)

    def pair_of(i):
        return (me // 2) ^ (2 * (i % (pairs // 2)) + 1 - i // (pairs // 2))

    def to_seq(src, dst, send_sem, recv_sem, peer, slot):
        return pltpu.make_async_remote_copy(
            src_ref=src.at[peer],
            dst_ref=dst.at[slot],
            send_sem=send_sem.at[peer],
            recv_sem=recv_sem.at[slot],
            device_id={"seq": peer},
            device_id_type=MESH,
        )

    def send_all(src, dst, send_sem, recv_sem):
        def step(i, carry):
            for side in range(2):
                peer = 2 * pair_of(i) + side

                @pl.when(peer != me)
                def _():
                    to_seq(src, dst, send_sem, recv_sem, peer, me).start()

            return carry

        lax.fori_loop(0, pairs, step, 0)

    def wait_all(src, dst, send_sem, recv_sem):
        def step(k, carry):
            copy = to_seq(src, dst, send_sem, recv_sem, me ^ k, me ^ k)
            copy.wait_send()
            copy.wait_recv()
            return carry

        lax.fori_loop(1, n_seq, step, 0)

    send_all(send_u, got_u, u_send, u_recv)
    send_all(send_v, got_v, v_send, v_recv)
    send_all(send_h, got_h, h_send, h_recv)
    send_all(send_c, got_c, c_send, c_recv)
    own = [
        pltpu.make_async_copy(src.at[me], dst.at[me], own_sem.at[i])
        for i, (src, dst) in enumerate(
            ((send_u, got_u), (send_h, got_h), (send_c, got_c), (send_v, got_v))
        )
    ]
    for copy in own:
        copy.start()

    def met_chan(k, carry):
        pl.semaphore_signal(met, inc=1, device_id={"chan": my_chan ^ k}, device_id_type=MESH)
        return carry

    lax.fori_loop(1, n_chan, met_chan, 0)
    loads[5].wait()
    loads[6].wait()
    flip = jnp.where(
        lax.broadcasted_iota(jnp.int32, (MINE, block), 1) < half, 1.0, -1.0
    ).astype(f32)

    def build(got, rows):
        def step(t, carry):
            x, y = (got[2 * t + i].astype(f32) for i in range(2))
            tile = jnp.concatenate([x, x * flip, y, y * flip], 0)
            rows[pl.ds(pl.multiple_of(t * 16, 16), 16), :] = tile.astype(bf16)
            return carry

        lax.fori_loop(0, pairs, step, 0)

    re = slice(0, LANES)
    im = slice(LANES, 2 * LANES)
    turn = (((1,), (1,)), ((), ()))
    upper = lax.broadcasted_iota(jnp.int32, (8, LANES), 0) < MINE
    scale = 1.0 / (block * 128.0)

    def times_table(lhs, j):
        return jnp.dot(lhs, high[j], preferred_element_type=f32) + jnp.dot(
            lhs, low[j], preferred_element_type=f32
        )

    def add(acc, term):
        return term if acc is None else (acc[0] + term[0], acc[1] + term[1])

    def fold(base, done, j, offset):
        for i in range(0, GROUP, 2):
            at = slice(offset + (base + i) * MINE, offset + (base + i) * MINE + 8)
            for lane, part in ((re, 0), (im, 1)):
                x, y = done[i][part], done[i + 1][part]
                rx, ry = pltpu.roll(x, MINE, axis=0), pltpu.roll(y, MINE, axis=0)
                sums[j, at, lane] = jnp.where(upper, x + rx, y + ry)
                diffs[j, at, lane] = jnp.where(upper, x - rx, ry - y)

    def correlate(p, q, sign, j, offset):
        after = None
        for base in reversed(range(0, n_seq, GROUP)):
            acc = [None] * GROUP
            for c in range(n_seq - base):
                pr, pi = p(c)
                for i in range(GROUP):
                    if base + i + c < n_seq:
                        qr, qi = q(base + i + c)
                        acc[i] = add(acc[i], (pr * qr + pi * qi, pr * qi - pi * qr))
            done = [None] * GROUP
            for i in reversed(range(GROUP)):
                zr, zi = acc[i]
                if after is None:
                    done[i] = (zr, zi)
                else:
                    done[i] = (zr + sign * after[1], zi - sign * after[0])
                after = (zr, zi)
            fold(base, done, j, offset)

    def convolve(p, q, sign, j, offset):
        before = None
        for base in range(0, n_seq, GROUP):
            acc = [None] * GROUP
            for c in range(base + GROUP):
                pr, pi = p(c)
                for i in range(GROUP):
                    if base + i - c >= 0:
                        qr, qi = q(base + i - c)
                        acc[i] = add(acc[i], (pr * qr - pi * qi, pr * qi + pi * qr))
            done = [None] * GROUP
            for i in range(GROUP):
                zr, zi = acc[i]
                if before is None:
                    done[i] = (zr, zi)
                else:
                    done[i] = (zr - sign * before[1], zi + sign * before[0])
                before = (zr, zi)
            fold(base, done, j, offset)

    def tiles_of(spectra, j):
        def tile(a):
            at = slice(a * 8, a * 8 + 8)
            return spectra[j, at, re], spectra[j, at, im]

        return tile

    small = n_seq * MINE

    own[0].wait()
    wait_all(send_u, got_u, u_send, u_recv)
    build(got_u, rows_u)

    def upstream_spectra(j, carry):
        spec_u[j] = times_table(rows_u[...], j)
        return carry

    lax.fori_loop(0, chunks, upstream_spectra, 0)
    own[3].wait()
    wait_all(send_v, got_v, v_send, v_recv)
    build(got_v, rows_v)
    spec_v[0] = times_table(rows_v[...], 0)
    for j in range(chunks):
        if j + 1 < chunks:
            spec_v[j + 1] = times_table(rows_v[...], j + 1)
        sign = 1.0 if j < chunks // 2 else -1.0
        correlate(tiles_of(spec_v, j), tiles_of(spec_u, j), sign, j, 0)
        packed_f[0, j] = sums[j, :small, :].astype(bf16)
        packed_f[1, j] = diffs[j, :small, :].astype(bf16)

    def back(packed, parity, start, tables):
        total = None
        at = pl.ds(pl.multiple_of(parity * half + start, WIDE), WIDE)
        for j in range(chunks):
            lhs = packed[parity, j]
            for table in tables:
                part = lax.dot_general(
                    lhs, table[j, at, :], turn, preferred_element_type=f32
                )
                total = part if total is None else total + part
        return total * scale

    def inverse_f(t, carry):
        for parity in range(2):
            grads = back(packed_f, parity, t * WIDE, (high,))
            for a in range(n_seq):
                part = grads[a * MINE : a * MINE + MINE]
                send_f[a, parity * (half // WIDE) + t] = part.astype(bf16)
        return carry

    lax.fori_loop(0, half // WIDE, inverse_f, 0)
    own_f = pltpu.make_async_copy(send_f.at[me], got_f.at[me], own_sem.at[4])
    own_f.start()
    send_all(send_f, got_f, f_send, f_recv)

    own[1].wait()
    wait_all(send_h, got_h, h_send, h_recv)

    build(got_h, rows_h)
    spec_h[0] = times_table(rows_h[...], 0)
    for j in range(chunks):
        if j + 1 < chunks:
            spec_h[j + 1] = times_table(rows_h[...], j + 1)
        sign = 1.0 if j < chunks // 2 else -1.0
        correlate(tiles_of(spec_h, j), tiles_of(spec_u, j), sign, j, 0)
        convolve(tiles_of(spec_h, j), tiles_of(spec_v, j), sign, j, small)
        packed_m[0, j] = sums[j].astype(bf16)
        packed_m[1, j] = diffs[j].astype(bf16)

    own[2].wait()
    wait_all(send_c, got_c, c_send, c_recv)
    pl.semaphore_wait(met, n_chan - 1)

    piece = share // 2
    lane_piece = lax.broadcasted_iota(jnp.int32, (8, LANES), 1) // piece
    per_tile = LANES // piece

    def to_owner(a, c):
        return pltpu.make_async_remote_copy(
            src_ref=send_t.at[a, c],
            dst_ref=tiles.at[my_chan, me],
            send_sem=t_send,
            recv_sem=t_recv,
            device_id={"seq": a, "chan": c},
            device_id_type=MESH,
        )

    def inverse_m(t, carry):
        for parity in range(2):
            signal_m[parity] = back(packed_m, parity, t * WIDE, (high, low))

        def finish(i, carry):
            pair = pair_of(i)
            at_v = pl.ds(pl.multiple_of(pair * 8, 8), 8)
            at_c = pl.ds(pl.multiple_of(small + pair * 8, 8), 8)
            parts = [signal_m[parity, at_v, :] for parity in range(2)]
            for parity in range(2):
                at = pl.ds(pl.multiple_of(parity * half + t * WIDE, WIDE), WIDE)
                cots = jnp.concatenate(
                    [got_c[2 * pair + side, :, at].astype(f32) for side in range(2)], 0
                )
                parts.append(signal_m[parity, at_c, :] * cots)
            for p in range(WIDE // LANES):
                lane = slice(p * LANES, (p + 1) * LANES)
                moved = [parts[0][:, lane]] + [
                    pltpu.roll(parts[n][:, lane], n * piece, axis=1) for n in range(1, 4)
                ]
                for q in range(per_tile):
                    out = moved[0]
                    for n in range(1, 4):
                        out = jnp.where(lane_piece == (q + n) % 4, moved[n], out)
                    c = (t * (WIDE // LANES) + p) * per_tile + q
                    for side in range(2):
                        part = out[side * MINE : side * MINE + MINE]
                        send_t[2 * pair + side, c] = part.astype(bf16)
            for q in range(WIDE // piece):
                c = t * (WIDE // piece) + q
                for side in range(2):
                    a = 2 * pair + side

                    @pl.when((a != me) | (c != my_chan))
                    def _():
                        to_owner(a, c).start()

            return carry

        lax.fori_loop(0, pairs, finish, 0)
        return carry

    lax.fori_loop(0, half // WIDE, inverse_m, 0)
    own_t = pltpu.make_async_copy(send_t.at[me, my_chan], tiles.at[my_chan, me], t_recv)
    own_t.start()

    own_f.wait()
    wait_all(send_f, got_f, f_send, f_recv)

    def unpack(i, carry):
        at = pl.ds(pl.multiple_of(i * 16, 16), 16)
        for t in range(block // WIDE):
            tile = [got_f[4 * i + n, t].astype(f32) for n in range(4)]
            lane = slice(t * WIDE, (t + 1) * WIDE)
            signal_f[at, lane] = jnp.concatenate(tile, 0).astype(bf16)
        return carry

    lax.fori_loop(0, n_seq // 4, unpack, 0)

    def join(t, carry):
        at = pl.ds(pl.multiple_of(t * WIDE, WIDE), WIDE)
        filter_grad[:, at] = lax.dot_general(
            signal_f[...], split[at, :], turn, preferred_element_type=f32
        )
        return carry

    lax.fori_loop(0, block // WIDE, join, 0)
    loads[7].wait()
    loads[8].wait()

    pltpu.make_async_copy(tiles, tiles, t_recv).wait()

    def restack(c, carry):
        for q in range(n_seq // 4):
            tile = jnp.concatenate(
                [tiles[c, 4 * q + i].astype(f32) for i in range(4)], 0
            )
            at = pl.ds(pl.multiple_of(c * 64 + q * 16, 16), 16)
            stacked[at, :] = tile.astype(bf16)
        return carry

    lax.fori_loop(0, n_chan, restack, 0)

    lane_of = lax.broadcasted_iota(jnp.int32, (LANES, LANES), 1)
    row_of = lax.broadcasted_iota(jnp.int32, (LANES, LANES), 0)
    source = (lane_of // piece + 4 - my_chan % 4) % 4
    wanted = (source // 2) * share + 2 * (lane_of % piece) + source % 2
    choice = jnp.where(row_of == wanted, 1.0, 0.0).astype(bf16)
    tokens = lax.dot_general(choice, stacked[...], turn, preferred_element_type=f32)
    tokens = tokens.astype(bf16)
    out = lax.dot_general(tokens[:share], wv[...], turn, preferred_element_type=f32)
    out = out + lax.dot_general(tokens[share:], wg[...], turn, preferred_element_type=f32)
    input_grad[...] = out.astype(bf16)

    def drain(k, carry):
        pltpu.make_async_copy(send_t.at[k], send_t.at[k], t_send).wait()
        return carry

    lax.fori_loop(1, n_seq, drain, 0)
    rest = send_t.at[0, pl.ds(0, n_chan - 1)]
    pltpu.make_async_copy(rest, rest, t_send).wait()


def solution(mesh):
    n_seq = mesh.shape["seq"]
    n_chan = mesh.shape["chan"]
    bf16 = jnp.bfloat16
    f32 = jnp.float32

    def local(values, gate_acts, cotangent, filter_taps, w_value, w_gate):
        channels, block = values.shape
        chunks = block // 2 // LANES
        model = w_value.shape[0]
        high, low, split = dft_tables(block)
        vmem = pl.BlockSpec(memory_space=pltpu.VMEM)
        hbm = pl.BlockSpec(memory_space=pltpu.MemorySpace.HBM)
        sems = pltpu.SemaphoreType.DMA
        return pl.pallas_call(
            functools.partial(kernel, n_seq, n_chan),
            out_shape=(
                jax.ShapeDtypeStruct((block // n_chan, model), bf16),
                jax.ShapeDtypeStruct((channels, block), f32),
            ),
            in_specs=[hbm] * 9,
            out_specs=(vmem, vmem),
            scratch_shapes=[
                pltpu.VMEM((channels, block), bf16),
                pltpu.VMEM((channels, block), bf16),
                pltpu.VMEM((channels, block), bf16),
                pltpu.VMEM((channels, block), f32),
                pltpu.VMEM((chunks, block, 2 * LANES), bf16),
                pltpu.VMEM((chunks, block, 2 * LANES), bf16),
                pltpu.VMEM((block, block), bf16),
                pltpu.VMEM((model, model), bf16),
                pltpu.VMEM((model, model), bf16),
                pltpu.VMEM((4 * channels, block), bf16),
                pltpu.VMEM((4 * channels, block), f32),
                pltpu.VMEM((n_seq, MINE, block), bf16),
                pltpu.VMEM((n_seq, MINE, block), bf16),
                pltpu.VMEM((n_seq, MINE, block), bf16),
                pltpu.VMEM((n_seq, MINE, block), bf16),
                pltpu.VMEM((n_seq, MINE, block), bf16),
                pltpu.VMEM((n_seq, MINE, block), bf16),
                pltpu.VMEM((n_seq, MINE, block), bf16),
                pltpu.VMEM((n_seq, MINE, block), bf16),
                pltpu.VMEM((n_seq * 8, block), bf16),
                pltpu.VMEM((n_seq * 8, block), bf16),
                pltpu.VMEM((n_seq * 8, block), bf16),
                pltpu.VMEM((chunks, n_seq * 8, 2 * LANES), f32),
                pltpu.VMEM((chunks, n_seq * 8, 2 * LANES), f32),
                pltpu.VMEM((chunks, n_seq * 8, 2 * LANES), f32),
                pltpu.VMEM((chunks, n_seq * 8, 2 * LANES), f32),
                pltpu.VMEM((chunks, n_seq * 8, 2 * LANES), f32),
                pltpu.VMEM((2, chunks, n_seq * 4, 2 * LANES), bf16),
                pltpu.VMEM((2, chunks, n_seq * 8, 2 * LANES), bf16),
                pltpu.VMEM((n_seq * 4, block), bf16),
                pltpu.VMEM((2, n_seq * 8, WIDE), f32),
                pltpu.VMEM((n_seq, n_chan, MINE, LANES), bf16),
                pltpu.VMEM((n_seq, block // WIDE, MINE, WIDE), bf16),
                pltpu.VMEM((n_seq, block // WIDE, MINE, WIDE), bf16),
                pltpu.VMEM((n_chan, n_seq, MINE, LANES), bf16),
                pltpu.VMEM((model, LANES), bf16),
                sems((9,)),
                sems((5,)),
            ]
            + [sems((n_seq,))] * 10
            + [sems, sems, pltpu.SemaphoreType.REGULAR],
            compiler_params=pltpu.CompilerParams(
                collective_id=0, has_side_effects=True, vmem_limit_bytes=67_043_328
            ),
        )(
            values,
            gate_acts,
            cotangent,
            filter_taps,
            jnp.asarray(high),
            jnp.asarray(low),
            jnp.asarray(split),
            w_value,
            w_gate,
        )

    return jax.shard_map(
        local,
        mesh=mesh,
        in_specs=(P("chan", "seq"), P("chan", "seq"), P("chan", "seq"), P("chan", "seq"), P(), P()),
        out_specs=(P(("seq", "chan"), None), P("chan", "seq")),
        check_vma=False,
    )
```

```python
import functools

import numpy as np

import jax
import jax.numpy as jnp
import ml_dtypes
from jax import lax
from jax.experimental import pallas as pl
from jax.experimental.pallas import tpu as pltpu
from jax.sharding import PartitionSpec as P

MESH = pl.DeviceIdType.MESH
LANES = 128
MINE = 4
GROUP = 4
WIDE = 256


def dft_tables(block):
    half = block // 2
    chunks = half // LANES
    order = np.concatenate([np.arange(0, half, 2), np.arange(1, half, 2)])
    token = np.concatenate([np.arange(0, block, 2), np.arange(1, block, 2)])
    steps = (2 * order + 1)[None, :] * token[:, None] % (4 * block)
    angle = np.pi * steps / (2 * block)
    table = np.stack([np.cos(angle), -np.sin(angle)]).reshape(2, block, chunks, LANES)
    table = table.transpose(2, 1, 0, 3).reshape(chunks, block, 2 * LANES)
    high = table.astype(ml_dtypes.bfloat16)
    low = (table - high.astype(np.float64)).astype(ml_dtypes.bfloat16)
    split = (np.arange(block)[:, None] == token[None, :]).astype(ml_dtypes.bfloat16)
    return high, low, split


def kernel(
    n_seq,
    n_chan,
    values_hbm,
    gates_hbm,
    cotangent_hbm,
    taps_hbm,
    high_hbm,
    low_hbm,
    split_hbm,
    wv_hbm,
    wg_hbm,
    input_grad,
    filter_grad_hbm,
    values,
    gates,
    cotangent,
    taps,
    high,
    low,
    split,
    wv,
    wg,
    mixed,
    flat,
    send_u,
    send_v,
    send_h,
    send_c,
    got_u,
    got_v,
    got_h,
    got_c,
    rows_u,
    rows_v,
    rows_h,
    spec_u,
    spec_v,
    spec_h,
    sums,
    diffs,
    packed_f,
    packed_m,
    signal_f,
    signal_m,
    send_t,
    send_f,
    got_f,
    tiles,
    stacked,
    filter_grad,
    load_sem,
    own_sem,
    u_send,
    u_recv,
    v_send,
    v_recv,
    h_send,
    h_recv,
    c_send,
    c_recv,
    f_send,
    f_recv,
    t_send,
    t_recv,
    met,
):
    f32 = jnp.float32
    bf16 = jnp.bfloat16
    me = lax.axis_index("seq")
    my_chan = lax.axis_index("chan")
    block = values.shape[1]
    half = block // 2
    chunks = half // LANES
    share = block // n_chan
    pairs = n_seq // 2

    loads = [
        pltpu.make_async_copy(src, dst, load_sem.at[i])
        for i, (src, dst) in enumerate(
            (
                (taps_hbm, taps),
                (values_hbm, values),
                (gates_hbm, gates),
                (cotangent_hbm, cotangent),
                (split_hbm, split),
                (high_hbm, high),
                (low_hbm, low),
                (wv_hbm, wv),
                (wg_hbm, wg),
            )
        )
    ]
    barrier = pltpu.get_barrier_semaphore()

    def greet_seq(k, carry):
        pl.semaphore_signal(
            barrier, inc=1, device_id={"seq": me ^ k}, device_id_type=MESH
        )
        return carry

    def greet_chan(k, carry):
        pl.semaphore_signal(
            barrier, inc=1, device_id={"chan": my_chan ^ k}, device_id_type=MESH
        )
        return carry

    for k in sorted(range(1, n_seq), key=lambda k: -(k & 2)):
        greet_seq(k, 0)
    lax.fori_loop(1, n_chan, greet_chan, 0)
    for load in loads:
        load.start()

    for load in loads[:4]:
        load.wait()
    channels = values.shape[0]
    mixed[0:channels, :] = taps[...].astype(bf16)
    mixed[channels : 2 * channels, :] = values[...]
    cot = cotangent[...]
    upstream = cot.astype(f32) * gates[...].astype(f32)
    mixed[2 * channels : 3 * channels, :] = upstream.astype(bf16)
    mixed[3 * channels : 4 * channels, :] = cot
    loads[4].wait()

    def divide(t, carry):
        at = pl.ds(pl.multiple_of(t * WIDE, WIDE), WIDE)
        flat[:, at] = jnp.dot(mixed[...], split[:, at], preferred_element_type=f32)
        return carry

    lax.fori_loop(0, block // WIDE, divide, 0)

    def pack(t, carry):
        h, v, u, c = (
            flat[pl.ds(pl.multiple_of(i * channels + t * 8, 8), 8), :] for i in range(4)
        )
        for side in range(2):
            part = slice(side * MINE, side * MINE + MINE)
            send_u[2 * t + side] = u[part].astype(bf16)
            send_v[2 * t + side] = v[part].astype(bf16)
            send_h[2 * t + side] = h[part].astype(bf16)
            send_c[2 * t + side] = c[part].astype(bf16)
        return carry

    lax.fori_loop(0, pairs, pack, 0)
    pl.semaphore_wait(barrier, n_seq + n_chan - 2)

    def pair_of(i):
        return (me // 2) ^ (2 * (i % (pairs // 2)) + 1 - i // (pairs // 2))

    def to_seq(src, dst, send_sem, recv_sem, peer, slot):
        return pltpu.make_async_remote_copy(
            src_ref=src.at[peer],
            dst_ref=dst.at[slot],
            send_sem=send_sem.at[peer],
            recv_sem=recv_sem.at[slot],
            device_id={"seq": peer},
            device_id_type=MESH,
        )

    def send_all(src, dst, send_sem, recv_sem):
        def step(i, carry):
            for side in range(2):
                peer = 2 * pair_of(i) + side

                @pl.when(peer != me)
                def _():
                    to_seq(src, dst, send_sem, recv_sem, peer, me).start()

            return carry

        lax.fori_loop(0, pairs, step, 0)

    def wait_all(src, dst, send_sem, recv_sem):
        def step(k, carry):
            copy = to_seq(src, dst, send_sem, recv_sem, me ^ k, me ^ k)
            copy.wait_send()
            copy.wait_recv()
            return carry

        lax.fori_loop(1, n_seq, step, 0)

    send_all(send_u, got_u, u_send, u_recv)
    send_all(send_v, got_v, v_send, v_recv)
    send_all(send_h, got_h, h_send, h_recv)
    send_all(send_c, got_c, c_send, c_recv)
    own = [
        pltpu.make_async_copy(src.at[me], dst.at[me], own_sem.at[i])
        for i, (src, dst) in enumerate(
            ((send_u, got_u), (send_h, got_h), (send_c, got_c), (send_v, got_v))
        )
    ]
    for copy in own:
        copy.start()

    def met_chan(k, carry):
        pl.semaphore_signal(met, inc=1, device_id={"chan": my_chan ^ k}, device_id_type=MESH)
        return carry

    lax.fori_loop(1, n_chan, met_chan, 0)
    loads[5].wait()
    loads[6].wait()
    flip = jnp.where(
        lax.broadcasted_iota(jnp.int32, (MINE, block), 1) < half, 1.0, -1.0
    ).astype(f32)

    def build(got, rows):
        def step(t, carry):
            x, y = (got[2 * t + i].astype(f32) for i in range(2))
            tile = jnp.concatenate([x, x * flip, y, y * flip], 0)
            rows[pl.ds(pl.multiple_of(t * 16, 16), 16), :] = tile.astype(bf16)
            return carry

        lax.fori_loop(0, pairs, step, 0)

    re = slice(0, LANES)
    im = slice(LANES, 2 * LANES)
    turn = (((1,), (1,)), ((), ()))
    upper = lax.broadcasted_iota(jnp.int32, (8, LANES), 0) < MINE
    scale = 1.0 / (block * 128.0)

    def times_table(lhs, j):
        return jnp.dot(lhs, high[j], preferred_element_type=f32) + jnp.dot(
            lhs, low[j], preferred_element_type=f32
        )

    def add(acc, term):
        return term if acc is None else (acc[0] + term[0], acc[1] + term[1])

    def fold(base, done, j, offset):
        for i in range(0, GROUP, 2):
            at = slice(offset + (base + i) * MINE, offset + (base + i) * MINE + 8)
            for lane, part in ((re, 0), (im, 1)):
                x, y = done[i][part], done[i + 1][part]
                rx, ry = pltpu.roll(x, MINE, axis=0), pltpu.roll(y, MINE, axis=0)
                sums[j, at, lane] = jnp.where(upper, x + rx, y + ry)
                diffs[j, at, lane] = jnp.where(upper, x - rx, ry - y)

    def correlate(p, q, sign, j, offset):
        after = None
        for base in reversed(range(0, n_seq, GROUP)):
            acc = [None] * GROUP
            for c in range(n_seq - base):
                pr, pi = p(c)
                for i in range(GROUP):
                    if base + i + c < n_seq:
                        qr, qi = q(base + i + c)
                        acc[i] = add(acc[i], (pr * qr + pi * qi, pr * qi - pi * qr))
            done = [None] * GROUP
            for i in reversed(range(GROUP)):
                zr, zi = acc[i]
                if after is None:
                    done[i] = (zr, zi)
                else:
                    done[i] = (zr + sign * after[1], zi - sign * after[0])
                after = (zr, zi)
            fold(base, done, j, offset)

    def convolve(p, q, sign, j, offset):
        before = None
        for base in range(0, n_seq, GROUP):
            acc = [None] * GROUP
            for c in range(base + GROUP):
                pr, pi = p(c)
                for i in range(GROUP):
                    if base + i - c >= 0:
                        qr, qi = q(base + i - c)
                        acc[i] = add(acc[i], (pr * qr - pi * qi, pr * qi + pi * qr))
            done = [None] * GROUP
            for i in range(GROUP):
                zr, zi = acc[i]
                if before is None:
                    done[i] = (zr, zi)
                else:
                    done[i] = (zr - sign * before[1], zi + sign * before[0])
                before = (zr, zi)
            fold(base, done, j, offset)

    def tiles_of(spectra, j):
        def tile(a):
            at = slice(a * 8, a * 8 + 8)
            return spectra[j, at, re], spectra[j, at, im]

        return tile

    small = n_seq * MINE

    own[0].wait()
    wait_all(send_u, got_u, u_send, u_recv)
    build(got_u, rows_u)

    def upstream_spectra(j, carry):
        spec_u[j] = times_table(rows_u[...], j)
        return carry

    lax.fori_loop(0, chunks, upstream_spectra, 0)
    own[3].wait()
    wait_all(send_v, got_v, v_send, v_recv)
    build(got_v, rows_v)
    spec_v[0] = times_table(rows_v[...], 0)
    for j in range(chunks):
        if j + 1 < chunks:
            spec_v[j + 1] = times_table(rows_v[...], j + 1)
        sign = 1.0 if j < chunks // 2 else -1.0
        correlate(tiles_of(spec_v, j), tiles_of(spec_u, j), sign, j, 0)
        packed_f[0, j] = sums[j, :small, :].astype(bf16)
        packed_f[1, j] = diffs[j, :small, :].astype(bf16)

    def back(packed, parity, start, tables):
        total = None
        at = pl.ds(pl.multiple_of(parity * half + start, WIDE), WIDE)
        for j in range(chunks):
            lhs = packed[parity, j]
            for table in tables:
                part = lax.dot_general(
                    lhs, table[j, at, :], turn, preferred_element_type=f32
                )
                total = part if total is None else total + part
        return total * scale

    def inverse_f(t, carry):
        for parity in range(2):
            grads = back(packed_f, parity, t * WIDE, (high,))
            for a in range(n_seq):
                part = grads[a * MINE : a * MINE + MINE]
                send_f[a, parity * (half // WIDE) + t] = part.astype(bf16)
        return carry

    lax.fori_loop(0, half // WIDE, inverse_f, 0)
    own_f = pltpu.make_async_copy(send_f.at[me], got_f.at[me], own_sem.at[4])
    own_f.start()
    send_all(send_f, got_f, f_send, f_recv)

    own[1].wait()
    wait_all(send_h, got_h, h_send, h_recv)

    build(got_h, rows_h)
    spec_h[0] = times_table(rows_h[...], 0)
    for j in range(chunks):
        if j + 1 < chunks:
            spec_h[j + 1] = times_table(rows_h[...], j + 1)
        sign = 1.0 if j < chunks // 2 else -1.0
        correlate(tiles_of(spec_h, j), tiles_of(spec_u, j), sign, j, 0)
        convolve(tiles_of(spec_h, j), tiles_of(spec_v, j), sign, j, small)
        packed_m[0, j] = sums[j].astype(bf16)
        packed_m[1, j] = diffs[j].astype(bf16)

    own[2].wait()
    wait_all(send_c, got_c, c_send, c_recv)
    pl.semaphore_wait(met, n_chan - 1)

    piece = share // 2
    lane_piece = lax.broadcasted_iota(jnp.int32, (8, LANES), 1) // piece
    per_tile = LANES // piece

    def to_owner(a, c):
        return pltpu.make_async_remote_copy(
            src_ref=send_t.at[a, c],
            dst_ref=tiles.at[my_chan, me],
            send_sem=t_send,
            recv_sem=t_recv,
            device_id={"seq": a, "chan": c},
            device_id_type=MESH,
        )

    def inverse_m(t, carry):
        for parity in range(2):
            signal_m[parity] = back(packed_m, parity, t * WIDE, (high, low))

        def finish(i, carry):
            pair = pair_of(i)
            at_v = pl.ds(pl.multiple_of(pair * 8, 8), 8)
            at_c = pl.ds(pl.multiple_of(small + pair * 8, 8), 8)
            parts = [signal_m[parity, at_v, :] for parity in range(2)]
            for parity in range(2):
                at = pl.ds(pl.multiple_of(parity * half + t * WIDE, WIDE), WIDE)
                cots = jnp.concatenate(
                    [got_c[2 * pair + side, :, at].astype(f32) for side in range(2)], 0
                )
                parts.append(signal_m[parity, at_c, :] * cots)
            for p in range(WIDE // LANES):
                lane = slice(p * LANES, (p + 1) * LANES)
                moved = [parts[0][:, lane]] + [
                    pltpu.roll(parts[n][:, lane], n * piece, axis=1) for n in range(1, 4)
                ]
                for q in range(per_tile):
                    out = moved[0]
                    for n in range(1, 4):
                        out = jnp.where(lane_piece == (q + n) % 4, moved[n], out)
                    c = (t * (WIDE // LANES) + p) * per_tile + q
                    for side in range(2):
                        part = out[side * MINE : side * MINE + MINE]
                        send_t[2 * pair + side, c] = part.astype(bf16)
            for q in range(WIDE // piece):
                c = t * (WIDE // piece) + q
                for side in range(2):
                    a = 2 * pair + side

                    @pl.when((a != me) | (c != my_chan))
                    def _():
                        to_owner(a, c).start()

            return carry

        lax.fori_loop(0, pairs, finish, 0)
        return carry

    lax.fori_loop(0, half // WIDE, inverse_m, 0)
    own_t = pltpu.make_async_copy(send_t.at[me, my_chan], tiles.at[my_chan, me], t_recv)
    own_t.start()

    own_f.wait()
    wait_all(send_f, got_f, f_send, f_recv)

    def unpack(i, carry):
        at = pl.ds(pl.multiple_of(i * 16, 16), 16)
        for t in range(block // WIDE):
            tile = [got_f[4 * i + n, t].astype(f32) for n in range(4)]
            lane = slice(t * WIDE, (t + 1) * WIDE)
            signal_f[at, lane] = jnp.concatenate(tile, 0).astype(bf16)
        return carry

    lax.fori_loop(0, n_seq // 4, unpack, 0)

    def join(t, carry):
        at = pl.ds(pl.multiple_of(t * WIDE, WIDE), WIDE)
        filter_grad[:, at] = lax.dot_general(
            signal_f[...], split[at, :], turn, preferred_element_type=f32
        )
        return carry

    lax.fori_loop(0, block // WIDE, join, 0)
    write_f = pltpu.make_async_copy(filter_grad, filter_grad_hbm, load_sem.at[9])
    write_f.start()
    loads[7].wait()
    loads[8].wait()

    pltpu.make_async_copy(tiles, tiles, t_recv).wait()

    def restack(c, carry):
        for q in range(n_seq // 4):
            tile = jnp.concatenate(
                [tiles[c, 4 * q + i].astype(f32) for i in range(4)], 0
            )
            at = pl.ds(pl.multiple_of(c * 64 + q * 16, 16), 16)
            stacked[at, :] = tile.astype(bf16)
        return carry

    lax.fori_loop(0, n_chan, restack, 0)

    lane_of = lax.broadcasted_iota(jnp.int32, (LANES, LANES), 1)
    row_of = lax.broadcasted_iota(jnp.int32, (LANES, LANES), 0)
    source = (lane_of // piece + 4 - my_chan % 4) % 4
    wanted = (source // 2) * share + 2 * (lane_of % piece) + source % 2
    choice = jnp.where(row_of == wanted, 1.0, 0.0).astype(bf16)
    tokens = lax.dot_general(choice, stacked[...], turn, preferred_element_type=f32)
    tokens = tokens.astype(bf16)
    out = lax.dot_general(tokens[:share], wv[...], turn, preferred_element_type=f32)
    out = out + lax.dot_general(tokens[share:], wg[...], turn, preferred_element_type=f32)
    input_grad[...] = out.astype(bf16)
    write_f.wait()

    def drain(k, carry):
        pltpu.make_async_copy(send_t.at[k], send_t.at[k], t_send).wait()
        return carry

    lax.fori_loop(1, n_seq, drain, 0)
    rest = send_t.at[0, pl.ds(0, n_chan - 1)]
    pltpu.make_async_copy(rest, rest, t_send).wait()


def solution(mesh):
    n_seq = mesh.shape["seq"]
    n_chan = mesh.shape["chan"]
    bf16 = jnp.bfloat16
    f32 = jnp.float32

    def local(values, gate_acts, cotangent, filter_taps, w_value, w_gate):
        channels, block = values.shape
        chunks = block // 2 // LANES
        model = w_value.shape[0]
        high, low, split = dft_tables(block)
        vmem = pl.BlockSpec(memory_space=pltpu.VMEM)
        hbm = pl.BlockSpec(memory_space=pltpu.MemorySpace.HBM)
        sems = pltpu.SemaphoreType.DMA
        return pl.pallas_call(
            functools.partial(kernel, n_seq, n_chan),
            out_shape=(
                jax.ShapeDtypeStruct((block // n_chan, model), bf16),
                jax.ShapeDtypeStruct((channels, block), f32),
            ),
            in_specs=[hbm] * 9,
            out_specs=(vmem, hbm),
            scratch_shapes=[
                pltpu.VMEM((channels, block), bf16),
                pltpu.VMEM((channels, block), bf16),
                pltpu.VMEM((channels, block), bf16),
                pltpu.VMEM((channels, block), f32),
                pltpu.VMEM((chunks, block, 2 * LANES), bf16),
                pltpu.VMEM((chunks, block, 2 * LANES), bf16),
                pltpu.VMEM((block, block), bf16),
                pltpu.VMEM((model, model), bf16),
                pltpu.VMEM((model, model), bf16),
                pltpu.VMEM((4 * channels, block), bf16),
                pltpu.VMEM((4 * channels, block), f32),
                pltpu.VMEM((n_seq, MINE, block), bf16),
                pltpu.VMEM((n_seq, MINE, block), bf16),
                pltpu.VMEM((n_seq, MINE, block), bf16),
                pltpu.VMEM((n_seq, MINE, block), bf16),
                pltpu.VMEM((n_seq, MINE, block), bf16),
                pltpu.VMEM((n_seq, MINE, block), bf16),
                pltpu.VMEM((n_seq, MINE, block), bf16),
                pltpu.VMEM((n_seq, MINE, block), bf16),
                pltpu.VMEM((n_seq * 8, block), bf16),
                pltpu.VMEM((n_seq * 8, block), bf16),
                pltpu.VMEM((n_seq * 8, block), bf16),
                pltpu.VMEM((chunks, n_seq * 8, 2 * LANES), f32),
                pltpu.VMEM((chunks, n_seq * 8, 2 * LANES), f32),
                pltpu.VMEM((chunks, n_seq * 8, 2 * LANES), f32),
                pltpu.VMEM((chunks, n_seq * 8, 2 * LANES), f32),
                pltpu.VMEM((chunks, n_seq * 8, 2 * LANES), f32),
                pltpu.VMEM((2, chunks, n_seq * 4, 2 * LANES), bf16),
                pltpu.VMEM((2, chunks, n_seq * 8, 2 * LANES), bf16),
                pltpu.VMEM((n_seq * 4, block), bf16),
                pltpu.VMEM((2, n_seq * 8, WIDE), f32),
                pltpu.VMEM((n_seq, n_chan, MINE, LANES), bf16),
                pltpu.VMEM((n_seq, block // WIDE, MINE, WIDE), bf16),
                pltpu.VMEM((n_seq, block // WIDE, MINE, WIDE), bf16),
                pltpu.VMEM((n_chan, n_seq, MINE, LANES), bf16),
                pltpu.VMEM((model, LANES), bf16),
                pltpu.VMEM((channels, block), f32),
                sems((10,)),
                sems((5,)),
            ]
            + [sems((n_seq,))] * 10
            + [sems, sems, pltpu.SemaphoreType.REGULAR],
            compiler_params=pltpu.CompilerParams(
                collective_id=0, has_side_effects=True, vmem_limit_bytes=67_043_328
            ),
        )(
            values,
            gate_acts,
            cotangent,
            filter_taps,
            jnp.asarray(high),
            jnp.asarray(low),
            jnp.asarray(split),
            w_value,
            w_gate,
        )

    return jax.shard_map(
        local,
        mesh=mesh,
        in_specs=(P("chan", "seq"), P("chan", "seq"), P("chan", "seq"), P("chan", "seq"), P(), P()),
        out_specs=(P(("seq", "chan"), None), P("chan", "seq")),
        check_vma=False,
    )
```
